128 devices in a mesh: row: 8 (over x, y_lo), col: 16 (over z, y_hi, core).
Axes of the slice: x: 4, y: 4 (y_hi: 2, y_lo: 2; y = y_hi * 2 + y_lo), z: 4, core: 2. Of those that a mesh axis runs over, the one named last changes fastest.
Arguments:
- tokens: bfloat16 [64, 256, 256], P('row', 'col'), may hold values from -18 to 18
- qkv_weight: bfloat16 [256, 768], replicated, may hold values from -0.375 to 0.375
- conv_weight: bfloat16 [25, 768], replicated, may hold values from -1.25 to 1.25
- proj_weight: bfloat16 [512, 256], replicated, may hold values from -0.25 to 0.25
- out_grad: bfloat16 [64, 256, 256], P('row', 'col'), may hold values from -6 to 6
Outputs:
- block_output: bfloat16 [64, 256, 256], P('row', 'col')
- input_grad: bfloat16 [64, 256, 256], P('row', 'col')
- qkv_grad: float32 [256, 768], replicated
- conv_grad: float32 [25, 768], replicated
- proj_grad: float32 [512, 256], replicated
The draws below stay inside these ranges and needn't reach their ends.
All inputs are finite; a program needn't handle non-finite values.
Results may differ from the reference program's by a relative error of at most 0.0085.
The reference program's roundings to bfloat16 on the way count: a program that leaves them out, or rounds other values in their place, can miss the bound.
Values may be sent and summed in bfloat16 or wider, within the bound.
No kernel may reach another device: no remote copies, remote signals or barrier semaphores. Data moves between devices by JAX's collectives and lax.ppermute only.
A program may use at most 64 MiB of HBM per device.

```python
import jax
import jax.numpy as jnp
from jax import lax

MODEL_WIDTH = 256
HEAD_COUNT = 8
HEAD_SIZE = 32
KERNEL_SIZE = 5
TILE_ROWS = 8
IMAGE_ROWS = 64
IMAGE_COLS = 256
TOKENS = 16384
N_ROW = 8


def draw_tokens(key, part):
    key_scale, key_noise = jax.random.split(key, 2)
    row_position = jnp.arange(IMAGE_ROWS, dtype=jnp.float32) / max(IMAGE_ROWS - 1, 1)
    col_position = jnp.arange(IMAGE_COLS, dtype=jnp.float32) / max(IMAGE_COLS - 1, 1)
    position_level = 0.5 * (row_position[:, None] + col_position[None, :])
    roughness = jax.random.uniform(key_scale, (IMAGE_ROWS, IMAGE_COLS), jnp.float32, -0.35, 0.35)
    magnitude = 0.3 * jnp.exp(jnp.log(10.0) * position_level + roughness)
    shape_full = (IMAGE_ROWS, IMAGE_COLS, MODEL_WIDTH)
    fluctuation = jnp.clip(jax.random.normal(key_noise, shape_full, jnp.float32), -4.0, 4.0)
    values = magnitude[:, :, None] * fluctuation
    return values.astype(jnp.bfloat16)


def steps_of(own_key, dims, pieces, least, top_value):
    level, own = 1.0, jax.random.fold_in(own_key, 6)
    for axis_at, shards_of in pieces:
        heights = jnp.exp(jax.random.uniform(jax.random.fold_in(own, axis_at), (shards_of,), jnp.float32, least / len(pieces), top_value / len(pieces)))
        level = level * jnp.repeat(heights, dims[axis_at] // shards_of).reshape([-1 if axis == axis_at else 1 for axis in range(len(dims))])
    return level


def noise(rng, shape, deviation, bound, pieces=(), kind=jnp.bfloat16):
    loudness = steps_of(rng, shape, pieces, -0.22, 0.18) if pieces else 1.0
    result = jax.random.normal(rng, shape, jnp.float32) * deviation * loudness
    return jnp.minimum(jnp.maximum(result, -bound), bound).astype(kind)


def setup_inputs(seed: int = 0) -> dict:
    key_of = jax.random.split(jax.random.key(seed), 6)
    return {
        "tokens": draw_tokens(jax.random.fold_in(key_of[5], 71), 0),
        "qkv_weight": noise(key_of[1], (MODEL_WIDTH, 3 * MODEL_WIDTH), MODEL_WIDTH ** -0.5, 0.375),
        "conv_weight": noise(key_of[2], (KERNEL_SIZE * KERNEL_SIZE, 3 * MODEL_WIDTH), (KERNEL_SIZE * KERNEL_SIZE) ** -0.5, 1.25),
        "proj_weight": noise(key_of[3], (2 * MODEL_WIDTH, MODEL_WIDTH), (2 * MODEL_WIDTH) ** -0.5, 0.25),
        "out_grad": noise(key_of[4], (IMAGE_ROWS, IMAGE_COLS, MODEL_WIDTH), 1.0, 6.0, ((0, 8), (1, 16))),
    }


PRECISE = lax.Precision.HIGHEST


def tap_sum(padded, kernel, flipped, extra):
    margin = (KERNEL_SIZE - 1) // 2
    channels = padded.shape[2]

    def row_block(block_index):
        block_start = (block_index * TILE_ROWS).astype(jnp.int32)
        slab_rows = lax.dynamic_slice_in_dim(padded, block_start, TILE_ROWS + 2 * margin, 0)
        accumulated = jnp.zeros((TILE_ROWS, IMAGE_COLS, channels), jnp.float32)
        if extra is not None:
            accumulated = accumulated + lax.dynamic_slice_in_dim(extra, block_start, TILE_ROWS, 0).astype(jnp.float32)
        for offset in range(KERNEL_SIZE * KERNEL_SIZE):
            down_shift = offset // KERNEL_SIZE
            side_shift = offset % KERNEL_SIZE
            if flipped:
                down_shift = 2 * margin - down_shift
                side_shift = 2 * margin - side_shift
            window = slab_rows[down_shift:down_shift + TILE_ROWS, side_shift:side_shift + IMAGE_COLS]
            accumulated = accumulated + window.astype(jnp.float32) * kernel[offset].astype(jnp.float32)
        return accumulated.astype(jnp.bfloat16)

    stacked = lax.map(row_block, jnp.arange(N_ROW, dtype=jnp.int32))
    return stacked.reshape(IMAGE_ROWS, IMAGE_COLS, channels)


def tap_products(padded, gradients):
    margin = (KERNEL_SIZE - 1) // 2

    def row_block(block_index):
        block_start = (block_index * TILE_ROWS).astype(jnp.int32)
        slab_rows = lax.dynamic_slice_in_dim(padded, block_start, TILE_ROWS + 2 * margin, 0)
        gradient_rows = lax.dynamic_slice_in_dim(gradients, block_start, TILE_ROWS, 0).astype(jnp.float32)
        sums = []
        for offset in range(KERNEL_SIZE * KERNEL_SIZE):
            down_shift = offset // KERNEL_SIZE
            side_shift = offset % KERNEL_SIZE
            window = slab_rows[down_shift:down_shift + TILE_ROWS, side_shift:side_shift + IMAGE_COLS]
            sums.append(jnp.sum(window.astype(jnp.float32) * gradient_rows, axis=(0, 1)))
        return jnp.stack(sums)

    return jnp.sum(lax.map(row_block, jnp.arange(N_ROW, dtype=jnp.int32)), axis=0)


def split_heads(base, aggregated, branch_index):
    lower = branch_index * MODEL_WIDTH
    joined = jnp.concatenate([base[:, lower:lower + MODEL_WIDTH], aggregated[:, lower:lower + MODEL_WIDTH]], axis=1)
    return joined.reshape(TOKENS, 2 * HEAD_COUNT, HEAD_SIZE).transpose(1, 0, 2)


def join_heads(stacked):
    return stacked.transpose(1, 0, 2).reshape(TOKENS, 2 * MODEL_WIDTH)


def head_forward(head_parts):
    query_raw, key_raw, value_raw = head_parts
    query_pos = jax.nn.relu(query_raw)
    key_pos = jax.nn.relu(key_raw)
    kv_state = jnp.dot(key_pos.T, value_raw, preferred_element_type=jnp.float32) / TOKENS
    key_mean = jnp.sum(key_pos.astype(jnp.float32), axis=0) / TOKENS
    query_float = query_pos.astype(jnp.float32)
    numerator = jnp.dot(query_float, kv_state, precision=PRECISE)
    denominator = jnp.dot(query_float, key_mean, precision=PRECISE) + 1.0
    return (numerator / denominator[:, None]).astype(jnp.bfloat16), kv_state, key_mean, denominator


def head_backward(head_parts):
    query_raw, key_raw, value_raw, kv_state, key_mean, denominator, att_grad = head_parts
    query_float = jax.nn.relu(query_raw).astype(jnp.float32)
    key_float = jax.nn.relu(key_raw).astype(jnp.float32)
    value_float = value_raw.astype(jnp.float32)
    numerator = jnp.dot(query_float, kv_state, precision=PRECISE)
    grad_float = att_grad.astype(jnp.float32)
    numerator_grad = grad_float / denominator[:, None]
    denominator_grad = -jnp.sum(grad_float * numerator, axis=1) / (denominator * denominator)
    state_grad = jnp.dot(query_float.T, numerator_grad, precision=PRECISE)
    mean_grad = jnp.dot(denominator_grad, query_float, precision=PRECISE)
    query_grad = jnp.dot(numerator_grad, kv_state.T, precision=PRECISE) + denominator_grad[:, None] * key_mean[None, :]
    key_grad = (jnp.dot(value_float, state_grad.T, precision=PRECISE) + mean_grad[None, :]) / TOKENS
    value_grad = jnp.dot(key_float, state_grad, precision=PRECISE) / TOKENS
    query_grad = jnp.where(query_raw > 0, query_grad, 0.0).astype(jnp.bfloat16)
    key_grad = jnp.where(key_raw > 0, key_grad, 0.0).astype(jnp.bfloat16)
    return query_grad, key_grad, value_grad.astype(jnp.bfloat16)


def reference(tokens, qkv_weight, conv_weight, proj_weight, out_grad):
    margin = (KERNEL_SIZE - 1) // 2
    pads = ((margin, margin), (margin, margin), (0, 0))
    flattened = tokens.reshape(TOKENS, MODEL_WIDTH)
    qkv_flat = jnp.dot(flattened, qkv_weight, preferred_element_type=jnp.float32).astype(jnp.bfloat16)
    qkv_image = qkv_flat.reshape(IMAGE_ROWS, IMAGE_COLS, 3 * MODEL_WIDTH)
    qkv_padded = jnp.pad(qkv_image, pads)
    aggregated = tap_sum(qkv_padded, conv_weight, False, None)
    aggregated_flat = aggregated.reshape(TOKENS, 3 * MODEL_WIDTH)
    queries = split_heads(qkv_flat, aggregated_flat, 0)
    keys_all = split_heads(qkv_flat, aggregated_flat, 1)
    values_all = split_heads(qkv_flat, aggregated_flat, 2)
    head_outs, kv_states, key_means, denominators = lax.map(head_forward, (queries, keys_all, values_all))
    attended = join_heads(head_outs)
    projected = jnp.dot(attended, proj_weight, preferred_element_type=jnp.float32)
    block_output = (flattened.astype(jnp.float32) + projected).astype(jnp.bfloat16)
    block_output = block_output.reshape(IMAGE_ROWS, IMAGE_COLS, MODEL_WIDTH)

    grad_flat = out_grad.reshape(TOKENS, MODEL_WIDTH)
    attended_grad = jnp.dot(grad_flat, proj_weight.T, preferred_element_type=jnp.float32).astype(jnp.bfloat16)
    proj_grad = jnp.dot(attended.T, grad_flat, preferred_element_type=jnp.float32)
    grad_heads = attended_grad.reshape(TOKENS, 2 * HEAD_COUNT, HEAD_SIZE).transpose(1, 0, 2)
    query_grads, key_grads, value_grads = lax.map(
        head_backward, (queries, keys_all, values_all, kv_states, key_means, denominators, grad_heads))
    query_flat = join_heads(query_grads)
    key_flat = join_heads(key_grads)
    value_flat = join_heads(value_grads)
    base_grad = jnp.concatenate([query_flat[:, :MODEL_WIDTH], key_flat[:, :MODEL_WIDTH], value_flat[:, :MODEL_WIDTH]], axis=1)
    aggregated_grad = jnp.concatenate([query_flat[:, MODEL_WIDTH:], key_flat[:, MODEL_WIDTH:], value_flat[:, MODEL_WIDTH:]], axis=1)
    aggregated_image = aggregated_grad.reshape(IMAGE_ROWS, IMAGE_COLS, 3 * MODEL_WIDTH)
    conv_grad = tap_products(qkv_padded, aggregated_image)
    base_image = base_grad.reshape(IMAGE_ROWS, IMAGE_COLS, 3 * MODEL_WIDTH)
    qkv_total_grad = tap_sum(jnp.pad(aggregated_image, pads), conv_weight, True, base_image)
    qkv_total_flat = qkv_total_grad.reshape(TOKENS, 3 * MODEL_WIDTH)
    qkv_grad = jnp.dot(flattened.T, qkv_total_flat, preferred_element_type=jnp.float32)
    back_flat = jnp.dot(qkv_total_flat, qkv_weight.T, preferred_element_type=jnp.float32)
    input_grad = (grad_flat.astype(jnp.float32) + back_flat).astype(jnp.bfloat16)
    input_grad = input_grad.reshape(IMAGE_ROWS, IMAGE_COLS, MODEL_WIDTH)
    return block_output, input_grad, qkv_grad, conv_grad, proj_grad
```

```python
import jax
import jax.numpy as jnp
from jax import lax
from jax.sharding import PartitionSpec as P

HEAD_SIZE = 32
KERNEL_SIZE = 5

PRECISE = lax.Precision.HIGHEST
F32 = jnp.float32
BF16 = jnp.bfloat16


def gather(block, axis):
    count = lax.axis_size(axis)
    copies = jnp.broadcast_to(block[None], (count,) + block.shape)
    return lax.all_to_all(copies, axis, 0, 0, tiled=True)


def sum_over(block, axis):
    return jnp.sum(gather(block, axis), axis=0)


def dot_last(left, right):
    return lax.dot_general(left, right, (((1,), (0,)), ((), ())), preferred_element_type=F32)


def dot_first(left, right, precision=None):
    return lax.dot_general(
        left, right, (((0,), (0,)), ((), ())), preferred_element_type=F32, precision=precision
    )


def dot_rows(left, right, precision=None):
    return lax.dot_general(
        left, right, (((1,), (1,)), ((), ())), preferred_element_type=F32, precision=precision
    )


def local(tokens, qkv_weight, conv_weight, proj_weight, out_grad):
    height, breadth, channels = tokens.shape
    heads = lax.axis_size("row")
    strips = lax.axis_size("col")
    head = lax.axis_index("row")
    rows = height * heads
    total = float(rows * breadth * strips)
    margin = (KERNEL_SIZE - 1) // 2
    count = rows * breadth
    size = HEAD_SIZE
    wide = 2 * margin

    both = gather(jnp.concatenate([tokens, out_grad], axis=2), "row")
    both = both.reshape(count, 2 * channels)
    tokens_all = both[:, :channels]
    grads_all = both[:, channels:]

    weight_heads = qkv_weight.reshape(channels, 3, heads, size)
    own_weight = lax.dynamic_index_in_dim(weight_heads, head, 2, False).reshape(channels, 3 * size)
    kernel_heads = conv_weight.reshape(KERNEL_SIZE**2, 3, heads, size)
    own_kernel = lax.dynamic_index_in_dim(kernel_heads, head, 2, False)
    own_kernel = own_kernel.reshape(KERNEL_SIZE**2, 3 * size).astype(F32)
    proj_heads = proj_weight.reshape(2, heads, size, channels).transpose(1, 0, 2, 3)
    proj_heads = proj_heads.reshape(heads, 2 * size, channels)
    own_proj = lax.dynamic_index_in_dim(proj_heads, head, 0, False)

    qkv = dot_last(tokens_all, own_weight).astype(BF16)
    att_grad = dot_rows(grads_all, own_proj).astype(BF16)

    sent = jnp.concatenate([qkv, att_grad[:, size:]], axis=1).reshape(rows, breadth, 4 * size)
    forward = [(i, i + 1) for i in range(strips - 1)]
    backward = [(i + 1, i) for i in range(strips - 1)]
    low = lax.ppermute(sent[:, breadth - wide :], "col", forward)
    high = lax.ppermute(sent[:, :wide], "col", backward)
    strip = jnp.concatenate([low, sent, high], axis=1)
    qkv_wide = jnp.pad(strip[:, :, : 3 * size], ((margin, margin), (0, 0), (0, 0))).astype(F32)
    span = breadth + 2 * margin
    aggregated = jnp.zeros((rows, span, 3 * size), F32)
    for tap in range(KERNEL_SIZE**2):
        down, side = divmod(tap, KERNEL_SIZE)
        aggregated = aggregated + qkv_wide[down : down + rows, side : side + span] * own_kernel[tap]
    aggregated = aggregated.astype(BF16)
    inner = aggregated[:, margin : margin + breadth].reshape(count, 3 * size)

    def state_of(part):
        key = jax.nn.relu(part[:, size : 2 * size])
        state = dot_first(key, part[:, 2 * size :])
        return jnp.concatenate([state, jnp.sum(key.astype(F32), axis=0)[None]], axis=0)

    states = jnp.stack([state_of(qkv), state_of(inner)])
    states = sum_over(states.reshape(-1), "col").reshape(2, size + 1, size) / total
    state, key_mean = states[:, :size], states[:, size]

    def terms(query_raw, grad, branch):
        query = jax.nn.relu(query_raw).astype(F32)
        grad = grad.astype(F32)
        numerator = jnp.dot(query, state[branch], precision=PRECISE)
        denominator = jnp.dot(query, key_mean[branch][:, None], precision=PRECISE) + 1.0
        numerator_grad = grad / denominator
        denominator_grad = -jnp.sum(grad * numerator, axis=1, keepdims=True)
        denominator_grad = denominator_grad / (denominator * denominator)
        return query, numerator, denominator, numerator_grad, denominator_grad

    base_terms = terms(qkv[:, :size], att_grad[:, :size], 0)
    extra_grad = strip[:, margin : margin + span, 3 * size :].reshape(rows * span, size)
    wide_flat = aggregated.reshape(rows * span, 3 * size)
    side_terms = terms(wide_flat[:, :size], extra_grad, 1)

    def inside(values):
        shaped = values.reshape(rows, span, -1)[:, margin : margin + breadth]
        return shaped.reshape(count, -1)

    side_inner = [inside(values) for values in side_terms]
    attended = jnp.concatenate(
        [
            (base_terms[1] / base_terms[2]).astype(BF16),
            (side_inner[1] / side_inner[2]).astype(BF16),
        ],
        axis=1,
    )

    def state_grad_of(parts):
        query, _, _, numerator_grad, denominator_grad = parts
        both_grads = dot_first(
            jnp.concatenate([numerator_grad, denominator_grad], axis=1), query, PRECISE
        )
        return both_grads

    grads = jnp.stack([state_grad_of(base_terms), state_grad_of(side_inner)])
    grads = sum_over(grads.reshape(-1), "col").reshape(2, size + 1, size)
    state_grad, mean_grad = grads[:, :size], grads[:, size]

    def head_grads(part, parts, branch):
        query_raw, key_raw = part[:, :size], part[:, size : 2 * size]
        value = part[:, 2 * size :].astype(F32)
        _, _, _, numerator_grad, denominator_grad = parts
        query_grad = dot_rows(numerator_grad, state[branch], PRECISE)
        query_grad = query_grad + denominator_grad * key_mean[branch]
        query_grad = jnp.where(query_raw > 0, query_grad, 0.0)
        key_grad = jnp.dot(value, state_grad[branch], precision=PRECISE) + mean_grad[branch]
        key_grad = jnp.where(key_raw > 0, key_grad / total, 0.0)
        key = jax.nn.relu(key_raw).astype(F32)
        value_grad = dot_rows(key, state_grad[branch], PRECISE) / total
        return jnp.concatenate([query_grad, key_grad, value_grad], axis=1).astype(BF16)

    base_grad = head_grads(qkv, base_terms, 0)
    side_grad = head_grads(wide_flat, side_terms, 1).reshape(rows, span, 3 * size)
    place = lax.axis_index("col") * breadth - margin + jnp.arange(span, dtype=jnp.int32)
    valid = (place >= 0) & (place < breadth * strips)
    side_grad = jnp.where(valid[None, :, None], side_grad, 0).astype(F32)
    side_inside = side_grad[:, margin : margin + breadth]
    sums = []
    spread = base_grad.astype(F32).reshape(rows, breadth, 3 * size)
    side_tall = jnp.pad(side_grad, ((margin, margin), (0, 0), (0, 0)))
    for tap in range(KERNEL_SIZE**2):
        down, side = divmod(tap, KERNEL_SIZE)
        window = qkv_wide[down : down + rows, margin + side : margin + side + breadth]
        sums.append(jnp.sum(window * side_inside, axis=(0, 1)))
        up, left = wide - down, wide - side
        spread = spread + side_tall[up : up + rows, left : left + breadth] * own_kernel[tap]
    conv_part = jnp.stack(sums)
    qkv_total = spread.astype(BF16).reshape(count, 3 * size)

    qkv_part = dot_first(qkv_total, tokens_all)
    proj_part = dot_first(attended, grads_all)
    conv_part = jnp.pad(conv_part, ((0, 7), (0, 0)))
    parts = jnp.concatenate(
        [
            qkv_part.reshape(strips, -1, 128),
            proj_part.reshape(strips, -1, 128),
            jnp.pad(conv_part, ((0, 0), (0, 32))).reshape(strips, -1, 128),
        ],
        axis=1,
    )
    parts = jnp.sum(lax.all_to_all(parts, "col", 0, 0, tiled=True), axis=0).astype(BF16)
    parts = gather(parts, "col")
    qkv_rows = 3 * size * channels // 128 // strips
    proj_rows = 2 * size * channels // 128 // strips
    flat = parts.reshape(-1)
    shared = jnp.broadcast_to(flat, (heads, flat.size))
    sent_back = jnp.concatenate(
        [shared, attended.reshape(heads, -1), qkv_total.reshape(heads, -1)], axis=1
    ).reshape(heads, -1, 128)
    back = lax.all_to_all(sent_back, "row", 0, 0, tiled=True).reshape(heads, -1)
    sums = back[:, : flat.size].reshape(heads, strips, -1, 128).astype(F32)
    at = flat.size
    att_size = height * breadth * 2 * size
    attended_own = back[:, at : at + att_size].reshape(heads, height * breadth, 2 * size)
    total_own = back[:, at + att_size :].reshape(heads, height * breadth, 3 * size)

    qkv_grad = sums[:, :, :qkv_rows].reshape(heads, 3, size, channels)
    qkv_grad = qkv_grad.transpose(3, 1, 0, 2).reshape(channels, 3 * channels)
    proj_grad = sums[:, :, qkv_rows : qkv_rows + proj_rows].reshape(heads, 2, size, channels)
    proj_grad = proj_grad.transpose(1, 0, 2, 3).reshape(2 * channels, channels)
    conv_grad = sums[:, :, qkv_rows + proj_rows :].reshape(heads, 32, 128)
    conv_grad = conv_grad[:, : KERNEL_SIZE**2, : 3 * size].reshape(heads, KERNEL_SIZE**2, 3, size)
    conv_grad = conv_grad.transpose(1, 2, 0, 3).reshape(KERNEL_SIZE**2, 3 * channels)

    attended_own = attended_own.transpose(1, 0, 2).reshape(height * breadth, 2 * channels)
    projected = dot_last(attended_own, proj_heads.reshape(2 * channels, channels))
    block_output = (tokens.reshape(-1, channels).astype(F32) + projected).astype(BF16)
    total_own = total_own.reshape(heads, height * breadth, 3, size).transpose(1, 2, 0, 3)
    back_flat = dot_rows(total_own.reshape(height * breadth, 3 * channels), qkv_weight)
    input_grad = (out_grad.reshape(-1, channels).astype(F32) + back_flat).astype(BF16)
    return (
        block_output.reshape(tokens.shape),
        input_grad.reshape(tokens.shape),
        qkv_grad,
        conv_grad,
        proj_grad,
    )


def solution(mesh):
    placed = (P("row", "col", None), P(), P(), P(), P("row", "col", None))
    return jax.shard_map(
        local,
        mesh=mesh,
        in_specs=placed,
        out_specs=(P("row", "col", None), P("row", "col", None), P(), P(), P()),
        check_vma=False,
    )
```

```python
import jax
import jax.numpy as jnp
from jax import lax
from jax.experimental import pallas as pl
from jax.experimental.pallas import tpu as pltpu
from jax.sharding import PartitionSpec as P

HEAD = 32
TAPS = 5
MARGIN = TAPS // 2
LANES = 4 * HEAD

F32 = jnp.float32
BF16 = jnp.bfloat16


def lane_of(shape):
    return lax.broadcasted_iota(jnp.int32, shape, len(shape) - 1)


def halves(x):
    high = x.astype(BF16)
    return high, (x - high.astype(F32)).astype(BF16)


def mm(left, right, contract=(1, 0)):
    dims = (((contract[0],), (contract[1],)), ((), ()))
    return lax.dot_general(left, right, dims, preferred_element_type=F32)


def relu(x):
    return jnp.maximum(x, jnp.zeros((), x.dtype))


def pair_up(base, side):
    lane = lane_of(base.shape)
    return jnp.where(lane < 64, pltpu.roll(side, 64, 1), base)


def tall(matrix, above=0):
    below = LANES - HEAD - above
    parts = [jnp.zeros((above, matrix.shape[1]), F32)] if above else []
    parts += [matrix, jnp.zeros((below, matrix.shape[1]), F32)]
    return jnp.concatenate(parts, axis=0)


def aggregate_kernel(sent, low, high, base, kern, wide, strip, pack):
    rows, cols, _ = sent.shape
    span = strip.shape[1]
    edge = jnp.zeros((MARGIN, span, LANES), F32)
    strip[0:MARGIN] = edge
    strip[MARGIN + rows : rows + 2 * MARGIN] = edge
    strip[MARGIN : MARGIN + rows, 0:cols] = sent[...].astype(F32)
    strip[MARGIN : MARGIN + rows, cols : cols + 4] = high[...].astype(F32)
    strip[MARGIN : MARGIN + rows, cols + 4 : cols + 8] = low[...].astype(F32)
    step = 4

    def conv(i, carry):
        block = strip[pl.ds(i * step, step + 2 * MARGIN)]
        total = jnp.zeros((step, span, LANES), F32)
        for b in range(TAPS):
            window = pltpu.roll(block, (MARGIN - b) % span, 1)
            for a in range(TAPS):
                tap = kern[pl.ds(a * TAPS + b, 1), :].reshape(1, 1, LANES)
                total = total + window[a : a + step] * tap
        at = pl.multiple_of(i * step * span, step * span)
        wide[pl.ds(at, step * span), :] = total.reshape(step * span, LANES).astype(BF16)
        return carry

    lax.fori_loop(0, rows // step, conv, 0)

    def outer(x):
        ones = jnp.where(lane_of(x.shape) >= 96, jnp.ones((), BF16), x)
        return mm(relu(x), ones, (0, 0))[HEAD : 2 * HEAD]

    def states(i, carry):
        base_sum, side_sum = carry
        at = pl.multiple_of(i * 8 * span, 8 * span)
        x = wide[pl.ds(at, 8 * span), :].astype(F32).reshape(8, span, LANES)[:, :cols]
        side_sum = side_sum + outer(x.reshape(8 * cols, LANES).astype(BF16))
        at = pl.multiple_of(i * 8 * cols, 8 * cols)
        base_sum = base_sum + outer(base[pl.ds(at, 8 * cols), :])
        return base_sum, side_sum

    zero = jnp.zeros((HEAD, LANES), F32)
    base_sum, side_sum = lax.fori_loop(0, rows // 8, states, (zero, zero))
    pack[...] = jnp.broadcast_to(pair_up(base_sum, side_sum)[None], pack.shape)


def forward_kernel(total, gathered, base, wide, base_y, side_y, base_att, side_att, maps, pack):
    span, cols = 24, 16
    states = jnp.sum(gathered[...], axis=0) * (1.0 / total)
    lane = lane_of(states.shape)

    def prepare(branch):
        if branch == 0:
            state, mean = pltpu.roll(states, 32, 1), states[:, 96:97]
        else:
            state, mean = pltpu.roll(states, 96, 1), states[:, 32:33]
        mean = jnp.broadcast_to(mean, states.shape)
        state = jnp.where(lane >= 96, state, 0.0)
        maps[branch] = jnp.where(lane == 95, mean, state)
        return halves(tall(jnp.concatenate([state, mean], axis=1)))

    def terms(x, factors, y_ref, att_ref, at, inner):
        query = relu(x)
        wide_x = x.astype(F32)
        spot = lane_of(wide_x.shape)
        products = mm(query, factors[0]) + mm(query, factors[1])
        numerator = products[:, :LANES]
        inverse = 1.0 / (products[:, LANES:] + 1.0)
        along = jnp.sum(jnp.where(spot >= 96, wide_x * numerator, 0.0), axis=1, keepdims=True)
        att_ref[pl.ds(at, x.shape[0]), :] = (numerator * inverse).astype(BF16)
        y = jnp.where(spot >= 96, wide_x * inverse, 0.0)
        y = jnp.where(spot == 95, -along * inverse * inverse, y)
        y_ref[pl.ds(at, x.shape[0]), :] = y
        if inner:
            shaped = y.reshape(-1, span, LANES)[:, :cols]
            y = shaped.reshape(-1, LANES)
            shaped = query.astype(F32).reshape(-1, span, LANES)[:, :cols]
            query = shaped.reshape(-1, LANES).astype(BF16)
        high, low = halves(y)
        return (mm(query, high, (0, 0)) + mm(query, low, (0, 0)))[:HEAD]

    base_factors, side_factors = prepare(0), prepare(1)

    def base_step(i, carry):
        at = pl.multiple_of(i * 256, 256)
        return carry + terms(base[pl.ds(at, 256), :], base_factors, base_y, base_att, at, False)

    def side_step(i, carry):
        at = pl.multiple_of(i * 192, 192)
        return carry + terms(wide[pl.ds(at, 192), :], side_factors, side_y, side_att, at, True)

    zero = jnp.zeros((HEAD, LANES), F32)
    base_sum = lax.fori_loop(0, base.shape[0] // 256, base_step, zero)
    side_sum = lax.fori_loop(0, wide.shape[0] // 192, side_step, zero)
    pack[...] = jnp.broadcast_to(pair_up(base_sum, side_sum)[None], pack.shape)


def query_kernel(base_y, side_y, maps, base_att, side_att, both, base_q, side_q, proj, side_own):
    span, cols = 24, 16
    channels = both.shape[1] // 2

    def query_grad(y_ref, out_ref, branch, size):
        map_high, map_low = halves(tall(maps[branch]))

        def step(i, carry):
            at = pl.multiple_of(i * size, size)
            high, low = halves(y_ref[pl.ds(at, size), :])
            out = mm(high, map_high, (1, 1)) + mm(low, map_high, (1, 1)) + mm(high, map_low, (1, 1))
            out_ref[pl.ds(at, size), :] = out
            return carry

        lax.fori_loop(0, y_ref.shape[0] // size, step, 0)

    query_grad(base_y, base_q, 0, 256)
    query_grad(side_y, side_q, 1, 192)

    def proj_step(i, carry):
        at = pl.multiple_of(i * 8 * span, 8 * span)
        x = side_att[pl.ds(at, 8 * span), :].astype(F32).reshape(8, span, LANES)[:, :cols]
        x = x.reshape(8 * cols, LANES).astype(BF16)
        at = pl.multiple_of(i * 8 * cols, 8 * cols)
        grads = both[pl.ds(at, 8 * cols), channels:]
        side_own[pl.ds(at, 8 * cols), :] = x
        base_sum = carry[0] + mm(base_att[pl.ds(at, 8 * cols), :], grads, (0, 0))[96:]
        side_sum = carry[1] + mm(x, grads, (0, 0))[96:]
        return base_sum, side_sum

    zero = jnp.zeros((HEAD, channels), F32)
    base_sum, side_sum = lax.fori_loop(0, both.shape[0] // 128, proj_step, (zero, zero))
    proj[0:HEAD] = base_sum
    proj[HEAD:] = side_sum


def backward_kernel(
    total, gathered, base, wide, base_q, side_q, strip, kern, valid, both, base_att, side_own,
    proj, tokens_out, att_out, parts, field, straight, sums,
):
    span, cols = 24, 16
    rows = base.shape[0] // cols
    channels = both.shape[1] // 2
    grads = jnp.sum(gathered[...], axis=0) * (1.0 / total)
    lane = lane_of(grads.shape)

    def prepare(branch):
        if branch == 0:
            state, mean = pltpu.roll(grads, 96, 1), grads[:, 95:96]
        else:
            state, mean = pltpu.roll(grads, 32, 1), grads[:, 31:32]
        state = jnp.where((lane >= 64) & (lane < 96), state, 0.0)
        upper = jnp.where(lane == 96, jnp.broadcast_to(mean, state.shape), state)
        turned = pltpu.roll(jnp.transpose(tall(upper)), 32, 1)
        return halves(turned + tall(state, HEAD))

    def masked(x, query_grad, factors):
        wide_x = x.astype(F32)
        spot = lane_of(wide_x.shape)
        left = jnp.where(spot < 64, relu(wide_x), jnp.where(spot < 96, wide_x, 1.0)).astype(BF16)
        out = mm(left, factors[0]) + mm(left, factors[1])
        out = jnp.where(spot < HEAD, query_grad, out)
        keep = ((wide_x > 0) | (spot >= 64)) & (spot < 96)
        return jnp.where(keep, out, 0.0).astype(BF16).astype(F32)

    base_factors, side_factors = prepare(0), prepare(1)
    edge = jnp.zeros((MARGIN, span, LANES), F32)
    field[0:MARGIN] = edge
    field[MARGIN + rows : rows + 2 * MARGIN] = edge
    inside = valid[...][None]

    def make(i, carry):
        at = pl.multiple_of(i * 8 * span, 8 * span)
        size = 8 * span
        out = masked(wide[pl.ds(at, size), :], side_q[pl.ds(at, size), :], side_factors)
        field[pl.ds(MARGIN + i * 8, 8)] = out.reshape(8, span, LANES) * inside
        at = pl.multiple_of(i * 8 * cols, 8 * cols)
        size = 8 * cols
        out = masked(base[pl.ds(at, size), :], base_q[pl.ds(at, size), :], base_factors)
        straight[pl.ds(i * 8, 8)] = out.reshape(8, cols, LANES)
        return carry

    lax.fori_loop(0, rows // 8, make, 0)
    step = 4

    def spread(i, carry):
        block = field[pl.ds(i * step, step + 2 * MARGIN)]
        out = straight[pl.ds(i * step, step)]
        for b in range(TAPS):
            window = pltpu.roll(block, (b - MARGIN) % span, 1)[:, :cols]
            for a in range(TAPS):
                up = 2 * MARGIN - a
                tap = kern[pl.ds(a * TAPS + b, 1), :].reshape(1, 1, LANES)
                out = out + window[up : up + step] * tap
        at = pl.multiple_of(i * step * cols, step * cols)
        size = step * cols
        out = out.reshape(size, LANES)
        out = jnp.where(lane_of(out.shape) < 96, out, base_att[pl.ds(at, size), :].astype(F32))
        tokens_out[pl.ds(at, size), :] = out.astype(BF16)
        return carry

    lax.fori_loop(0, rows // step, spread, 0)

    def taps(i, carry):
        block = strip[pl.ds(i * step, step + 2 * MARGIN)]
        own = field[pl.ds(MARGIN + i * step, step)][:, :cols]
        found = list(carry)
        for b in range(TAPS):
            window = pltpu.roll(block, (MARGIN - b) % span, 1)[:, :cols]
            for a in range(TAPS):
                product = (window[a : a + step] * own).reshape(step * cols // 8, 8, LANES)
                k = a * TAPS + b
                found[k] = found[k] + jnp.sum(product, axis=0)
        return tuple(found)

    zero = jnp.zeros((8, LANES), F32)
    found = lax.fori_loop(0, rows // step, taps, (zero,) * TAPS**2)
    sums[...] = jnp.zeros(sums.shape, F32)
    for k in range(TAPS**2):
        sums[k : k + 1, :] = jnp.sum(found[k], axis=0, keepdims=True)

    def outer(i, carry):
        at = pl.multiple_of(i * 256, 256)
        return carry + mm(tokens_out[pl.ds(at, 256), :], both[pl.ds(at, 256), :channels], (0, 0))

    weight = lax.fori_loop(0, rows * cols // 256, outer, jnp.zeros((LANES, channels), F32))
    parts[0:96] = weight[:96, :LANES]
    parts[96:192] = weight[:96, LANES:]
    parts[192:256] = proj[:, :LANES]
    parts[256:320] = proj[:, LANES:]
    parts[320:352] = sums[...]
    parts[352:384] = jnp.zeros((32, LANES), F32)

    def pack(i, carry):
        at = pl.multiple_of(i * 128, 128)
        x = side_own[pl.ds(at, 128), :].astype(F32)
        out = jnp.zeros((32, LANES), F32)
        spot = lane_of(out.shape)
        for g in range(4):
            turned = pltpu.roll(x[32 * g : 32 * g + 32], (32 * g + 32) % LANES, 1)
            out = jnp.where((spot >= 32 * g) & (spot < 32 * g + 32), turned, out)
        att_out[i] = out.astype(BF16)
        return carry

    lax.fori_loop(0, rows // 8, pack, 0)


def finish_kernel(back, tokens, grads, weights, proj, block_out, input_out):
    heads = back.shape[0]
    block = tokens[...].astype(F32)
    inputs = grads[...].astype(F32)
    attended = jnp.zeros(block.shape, F32)
    turned = jnp.zeros(block.shape, F32)
    for h in range(heads):
        first = back[h, 0:128, :]
        turned = turned + mm(first, weights[h])
        packed = back[h, 128:160, :].astype(F32)
        side = jnp.concatenate([pltpu.roll(packed, 96 - 32 * g, 1) if g < 3 else packed for g in range(4)], axis=0)
        spot = lane_of(side.shape)
        both = jnp.where(spot >= 96, side, pltpu.roll(first.astype(F32), 96, 1))
        both = jnp.where(spot >= 64, both, 0.0).astype(BF16)
        attended = attended + mm(both, proj[h])
    block_out[...] = (block + attended).astype(BF16)
    input_out[...] = (inputs + turned).astype(BF16)


def assemble_kernel(sums, qkv_grad, conv_grad, proj_grad, scratch):
    heads = sums.shape[2]
    for h in range(heads):
        for part in range(16):
            scratch[h, 24 * part : 24 * part + 24, :] = sums[part // 2, part % 2, h].astype(F32)
    for j in range(3):
        for half in range(2):
            for quad in range(heads // 4):
                rows = [
                    scratch[4 * quad + h, 96 * half + 32 * j : 96 * half + 32 * j + 32, :]
                    for h in range(4)
                ]
                block = jnp.transpose(jnp.concatenate(rows, axis=0))
                at = 256 * j + 128 * quad
                qkv_grad[128 * half : 128 * half + 128, at : at + 128] = block
    for j in range(3):
        for quad in range(heads // 4):
            out = jnp.zeros((32, LANES), F32)
            spot = lane_of(out.shape)
            for h in range(4):
                turned = scratch[4 * quad + h, 320:352, :]
                if (h - j) % 4:
                    turned = pltpu.roll(turned, (32 * (h - j)) % LANES, 1)
                out = jnp.where((spot >= 32 * h) & (spot < 32 * h + 32), turned, out)
            at = 256 * j + 128 * quad
            conv_grad[:, at : at + 128] = out[: TAPS**2]
    for h in range(heads):
        for branch in range(2):
            at = 256 * branch + 32 * h
            for half in range(2):
                row = 192 + 64 * half + 32 * branch
                proj_grad[at : at + 32, 128 * half : 128 * half + 128] = scratch[h, row : row + 32, :]


def call(kernel, outs, *args, scratch=(), name=None):
    shapes = [jax.ShapeDtypeStruct(shape, dtype) for shape, dtype in outs]
    return pl.pallas_call(kernel, out_shape=shapes, scratch_shapes=list(scratch), name=name)(*args)


def exchange(block, axis, groups=None):
    return lax.all_to_all(block, axis, 0, 0, tiled=True, axis_index_groups=groups)


def copies(block, count):
    return jnp.broadcast_to(block[None], (count,) + block.shape)


def local(tokens, qkv_weight, conv_weight, proj_weight, out_grad):
    height, cols, channels = tokens.shape
    heads = lax.axis_size("row")
    strips = lax.axis_size("col")
    head = lax.axis_index("row")
    place = lax.axis_index("col")
    rows = height * heads
    total = float(rows * cols * strips)
    count = rows * cols
    span = cols + 4 * MARGIN

    both = exchange(copies(jnp.concatenate([tokens, out_grad], axis=2), heads), "row")
    both = both.reshape(count, 2 * channels)

    qkv_heads = qkv_weight.reshape(channels, 3, heads, HEAD).transpose(2, 0, 1, 3)
    qkv_heads = qkv_heads.reshape(heads, channels, 3 * HEAD)
    own_qkv = lax.dynamic_index_in_dim(qkv_heads, head, 0, False)
    own_kernel = conv_weight.reshape(TAPS**2, 3, heads, HEAD)
    own_kernel = lax.dynamic_index_in_dim(own_kernel, head, 2, False).reshape(TAPS**2, 3 * HEAD)
    centre = (jnp.arange(TAPS**2) == TAPS**2 // 2).astype(F32)
    kern = jnp.concatenate(
        [own_kernel.astype(F32), jnp.broadcast_to(centre[:, None], (TAPS**2, HEAD))], axis=1
    )
    proj_heads = proj_weight.reshape(2, heads, HEAD, channels).transpose(1, 0, 2, 3)
    proj_heads = proj_heads.reshape(heads, 2 * HEAD, channels)
    own_proj = lax.dynamic_index_in_dim(proj_heads, head, 0, False)
    blank = jnp.zeros((channels, HEAD), BF16)
    blanks = jnp.zeros((channels, 3 * HEAD), BF16)
    upper = jnp.concatenate([own_qkv, blank], axis=1)
    side_map = jnp.concatenate([upper, jnp.concatenate([blanks, own_proj[HEAD:].T], axis=1)])
    base_map = jnp.concatenate([upper, jnp.concatenate([blanks, own_proj[:HEAD].T], axis=1)])
    sent = mm(both, side_map).astype(BF16).reshape(rows, cols, LANES)
    base = mm(both, base_map).astype(BF16)

    forward = [(i, i + 1) for i in range(strips - 1)]
    backward = [(i + 1, i) for i in range(strips - 1)]
    low = lax.ppermute(sent[:, cols - 4 :], "col", forward)
    high = lax.ppermute(sent[:, :4], "col", backward)

    vast = rows * span
    small = (strips, HEAD, LANES)
    wide, strip, pack = call(
        aggregate_kernel,
        [((vast, LANES), BF16), ((rows + 4, span, LANES), F32), (small, F32)],
        sent, low, high, base, kern, name="aggregate",
    )
    gathered = exchange(pack, "col")
    base_y, side_y, base_att, side_att, maps, pack = call(
        lambda *refs: forward_kernel(total, *refs),
        [
            ((count, LANES), F32),
            ((vast, LANES), F32),
            ((count, LANES), BF16),
            ((vast, LANES), BF16),
            ((2, HEAD, LANES), F32),
            (small, F32),
        ],
        gathered, base, wide, name="forward",
    )
    gathered = exchange(pack, "col")
    base_q, side_q, proj, side_own = call(
        query_kernel,
        [
            ((count, LANES), F32),
            ((vast, LANES), F32),
            ((2 * HEAD, channels), F32),
            ((count, LANES), BF16),
        ],
        base_y, side_y, maps, base_att, side_att, both, name="query",
    )
    circle = jnp.arange(span, dtype=jnp.int32)
    shift = jnp.where(circle < cols + 4, circle, circle - span)
    at = place * cols + shift
    valid = (at >= 0) & (at < strips * cols) & (shift >= -MARGIN) & (shift < cols + MARGIN)
    valid = jnp.broadcast_to(valid.astype(F32)[:, None], (span, LANES))
    tokens_out, att_out, parts = call(
        lambda *refs: backward_kernel(total, *refs),
        [((count, LANES), BF16), ((heads, 32, LANES), BF16), ((384, LANES), F32)],
        gathered, base, wide, base_q, side_q, strip, kern, valid, both, base_att, side_own, proj,
        scratch=[
            pltpu.VMEM((rows + 4, span, LANES), F32),
            pltpu.VMEM((rows, cols, LANES), F32),
            pltpu.VMEM((32, LANES), F32),
        ],
        name="backward",
    )
    part = exchange(parts.reshape(strips, 24, LANES), "col")
    part = jnp.sum(part, axis=0).astype(BF16)
    sent_back = jnp.concatenate(
        [tokens_out.reshape(heads, -1, LANES), att_out, copies(part, heads)], axis=1
    )
    back = exchange(sent_back, "row")
    sums = back[:, 160:]
    other = lax.ppermute(sums, "col", [(i, i ^ 1) for i in range(strips)])
    even = place % 2 == 0
    sums = jnp.stack([jnp.where(even, sums, other), jnp.where(even, other, sums)])
    groups = [[2 * i + c for i in range(strips // 2)] for c in range(2)]
    sums = exchange(copies(sums, strips // 2), "col", groups)

    weights = jnp.pad(qkv_heads.transpose(0, 2, 1), ((0, 0), (0, HEAD), (0, 0)))
    proj_rows = jnp.pad(proj_heads, ((0, 0), (2 * HEAD, 0), (0, 0)))
    block_output, input_grad = call(
        finish_kernel,
        [((height * cols, channels), BF16)] * 2,
        back, tokens.reshape(-1, channels), out_grad.reshape(-1, channels), weights, proj_rows,
        name="finish",
    )
    qkv_grad, conv_grad, proj_grad = call(
        assemble_kernel,
        [
            ((channels, 3 * channels), F32),
            ((TAPS**2, 3 * channels), F32),
            ((2 * channels, channels), F32),
        ],
        sums, scratch=[pltpu.VMEM((heads, 384, LANES), F32)], name="assemble",
    )
    return (
        block_output.reshape(tokens.shape),
        input_grad.reshape(tokens.shape),
        qkv_grad,
        conv_grad,
        proj_grad,
    )


def solution(mesh):
    placed = (P("row", "col", None), P(), P(), P(), P("row", "col", None))
    return jax.shard_map(
        local,
        mesh=mesh,
        in_specs=placed,
        out_specs=(P("row", "col", None), P("row", "col", None), P(), P(), P()),
        check_vma=False,
    )
```

```python
import jax
import jax.numpy as jnp
from jax import lax
from jax.experimental import pallas as pl
from jax.experimental.pallas import tpu as pltpu
from jax.sharding import PartitionSpec as P

HEAD = 32
TAPS = 5
MARGIN = TAPS // 2
LANES = 4 * HEAD
GRANT = 16 * 2**20

F32 = jnp.float32
BF16 = jnp.bfloat16


def lane_of(shape):
    return lax.broadcasted_iota(jnp.int32, shape, len(shape) - 1)


def halves(x):
    high = x.astype(BF16)
    return high, (x - high.astype(F32)).astype(BF16)


def mm(left, right, contract=(1, 0)):
    dims = (((contract[0],), (contract[1],)), ((), ()))
    return lax.dot_general(left, right, dims, preferred_element_type=F32)


def relu(x):
    return jnp.maximum(x, jnp.zeros((), x.dtype))


def pair_up(base, side):
    lane = lane_of(base.shape)
    return jnp.where(lane < 64, pltpu.roll(side, 64, 1), base)


def tall(matrix, above=0):
    below = LANES - HEAD - above
    parts = [jnp.zeros((above, matrix.shape[1]), F32)] if above else []
    parts += [matrix, jnp.zeros((below, matrix.shape[1]), F32)]
    return jnp.concatenate(parts, axis=0)


def move(source, target, sem):
    copy = pltpu.make_async_copy(source, target, sem)
    copy.start()
    return copy


def spread_kernel(tokens, grads, out, buffer, sems):
    channels = tokens.shape[2]
    first = move(tokens, buffer.at[:, :, 0:channels], sems.at[0])
    second = move(grads, buffer.at[:, :, channels : 2 * channels], sems.at[1])
    first.wait()
    second.wait()
    moves = [move(buffer, out.at[i], sems.at[2 + i]) for i in range(out.shape[0])]
    for copy in moves:
        copy.wait()


def aggregate_kernel(sent, near, far, base, kern, inner, halo, strip_out, pack, strip, sems):
    rows, cols, _ = sent.shape
    span = strip.shape[1]
    even = lax.rem(lax.axis_index("col"), 2) == 0
    low = jnp.where(even, far[...].astype(F32), near[...].astype(F32))
    high = jnp.where(even, near[...].astype(F32), far[...].astype(F32))
    edge = jnp.zeros((MARGIN, span, LANES), F32)
    strip[0:MARGIN] = edge
    strip[MARGIN + rows : rows + 2 * MARGIN] = edge
    strip[MARGIN : MARGIN + rows, 0:cols] = sent[...].astype(F32)
    strip[MARGIN : MARGIN + rows, cols : cols + 4] = high
    strip[MARGIN : MARGIN + rows, cols + 4 : cols + 8] = low
    strip_move = move(strip, strip_out, sems.at[0])
    step = 4

    def conv(i, carry):
        block = strip[pl.ds(i * step, step + 2 * MARGIN)]
        total = jnp.zeros((step, span, LANES), F32)
        for b in range(TAPS):
            window = pltpu.roll(block, (MARGIN - b) % span, 1)
            for a in range(TAPS):
                tap = kern[pl.ds(a * TAPS + b, 1), :].reshape(1, 1, LANES)
                total = total + window[a : a + step] * tap
        size = step * cols
        at = pl.multiple_of(i * size, size)
        inner[pl.ds(at, size), :] = total[:, :cols].reshape(size, LANES).astype(BF16)
        size = step * (span - cols)
        at = pl.multiple_of(i * size, size)
        halo[pl.ds(at, size), :] = total[:, cols:].reshape(size, LANES).astype(BF16)
        return carry

    lax.fori_loop(0, rows // step, conv, 0)

    def outer(x):
        ones = jnp.where(lane_of(x.shape) >= 96, jnp.ones((), BF16), x)
        return mm(relu(x), ones, (0, 0))[HEAD : 2 * HEAD]

    def states(i, carry):
        at = pl.multiple_of(i * 256, 256)
        base_sum = carry[0] + outer(base[pl.ds(at, 256), :])
        side_sum = carry[1] + outer(inner[pl.ds(at, 256), :])
        return base_sum, side_sum

    zero = jnp.zeros((HEAD, LANES), F32)
    base_sum, side_sum = lax.fori_loop(0, rows * cols // 256, states, (zero, zero))
    pack[...] = jnp.broadcast_to(pair_up(base_sum, side_sum)[None], pack.shape)
    strip_move.wait()


def token_terms(x, factor):
    query = relu(x)
    wide = x.astype(F32)
    spot = lane_of(wide.shape)
    products = mm(jnp.concatenate([query, query], axis=1), factor)
    numerator = products[:, :LANES]
    inverse = 1.0 / (products[:, LANES:] + 1.0)
    along = jnp.sum(jnp.where(spot >= 96, wide * numerator, 0.0), axis=1, keepdims=True)
    y = jnp.where(spot >= 96, wide * inverse, 0.0)
    y = jnp.where(spot == 95, -along * inverse * inverse, y)
    return query, numerator * inverse, y


def forward_kernel(
    total, gathered, base, inner, y_out, att_out, maps_out, factor_out, pack_out,
    y, att, maps, factor, pack, sems,
):
    states = jnp.sum(gathered[...], axis=0) * (1.0 / total)
    lane = lane_of(states.shape)

    def prepare(branch):
        if branch == 0:
            state, mean = pltpu.roll(states, 32, 1), states[:, 96:97]
        else:
            state, mean = pltpu.roll(states, 96, 1), states[:, 32:33]
        mean = jnp.broadcast_to(mean, states.shape)
        state = jnp.where(lane >= 96, state, 0.0)
        maps[branch] = jnp.where(lane == 95, mean, state)
        return jnp.concatenate(halves(tall(jnp.concatenate([state, mean], axis=1))), axis=0)

    def walk(ref, factors, branch):
        def step(i, carry):
            at = pl.multiple_of(i * 256, 256)
            query, out, own = token_terms(ref[pl.ds(at, 256), :], factors)
            att[branch, pl.ds(at, 256), :] = out.astype(BF16)
            y[branch, pl.ds(at, 256), :] = own
            return carry + mm(query, jnp.concatenate(halves(own), axis=1), (0, 0))[:HEAD]

        found = lax.fori_loop(0, ref.shape[0] // 256, step, jnp.zeros((HEAD, 2 * LANES), F32))
        return found[:, :LANES] + found[:, LANES:]

    base_factor, side_factor = prepare(0), prepare(1)
    factor[...] = side_factor
    moves = [move(maps, maps_out, sems.at[0]), move(factor, factor_out, sems.at[1])]
    base_sum = walk(base, base_factor, 0)
    moves += [move(y.at[0], y_out.at[0], sems.at[2]), move(att.at[0], att_out.at[0], sems.at[3])]
    side_sum = walk(inner, side_factor, 1)
    moves += [move(y.at[1], y_out.at[1], sems.at[4]), move(att.at[1], att_out.at[1], sems.at[5])]
    pack[...] = pair_up(base_sum, side_sum)
    moves += [move(pack, pack_out.at[i], sems.at[6 + i]) for i in range(pack_out.shape[0])]
    for copy in moves:
        copy.wait()


def query_kernel(
    base, inner, halo, both, y_in, maps_in, factor_in, att_in, q_out, halo_out, proj_out,
    y, maps, factor, att, q, halo_q, proj, sems,
):
    channels = both.shape[1] // 2
    moves = [
        move(maps_in, maps, sems.at[0]),
        move(factor_in, factor, sems.at[1]),
        move(y_in, y, sems.at[2]),
        move(att_in, att, sems.at[3]),
    ]
    for copy in moves:
        copy.wait()

    def prepare(branch):
        high, low = halves(tall(maps[branch]))
        return jnp.concatenate([high, high], axis=1), low

    def query_grad(x, y, parts):
        high, low = halves(y)
        out = mm(jnp.concatenate([high, low], axis=1), parts[0], (1, 1)) + mm(high, parts[1], (1, 1))
        return jnp.where(x.astype(F32) > 0, out, 0.0).astype(BF16)

    for branch, ref in enumerate((base, inner)):
        parts = prepare(branch)

        def step(i, carry):
            at = pl.multiple_of(i * 256, 256)
            x = ref[pl.ds(at, 256), :]
            q[branch, pl.ds(at, 256), :] = query_grad(x, y[branch, pl.ds(at, 256), :], parts)
            grads = both[pl.ds(at, 256), channels:]
            return carry + mm(att[branch, pl.ds(at, 256), :], grads, (0, 0))[96:]

        zero = jnp.zeros((HEAD, channels), F32)
        found = lax.fori_loop(0, ref.shape[0] // 256, step, zero)
        proj[HEAD * branch : HEAD * branch + HEAD] = found

    parts = prepare(1)

    def edge(i, carry):
        at = pl.multiple_of(i * 256, 256)
        x = halo[pl.ds(at, 256), :]
        halo_q[pl.ds(at, 256), :] = query_grad(x, token_terms(x, factor[...])[2], parts)
        return carry

    lax.fori_loop(0, halo.shape[0] // 256, edge, 0)
    moves = [
        move(q, q_out, sems.at[0]),
        move(halo_q, halo_out, sems.at[1]),
        move(proj, proj_out, sems.at[2]),
    ]
    for copy in moves:
        copy.wait()


def backward_kernel(
    total, gathered, base, inner, halo, kern, both, q_from, halo_from, att_from, strip_from, proj_from,
    tokens_out, att_out, parts, q_in, halo_q, att, strip, proj, field, straight, sums, sems,
):
    q_move = move(q_from, q_in, sems.at[0])
    halo_move = move(halo_from, halo_q, sems.at[1])
    att_move = move(att_from, att, sems.at[2])
    strip_move = move(strip_from, strip, sems.at[3])
    proj_move = move(proj_from, proj, sems.at[4])
    span = strip.shape[1]
    rows = strip.shape[0] - 2 * MARGIN
    cols = base.shape[0] // rows
    channels = both.shape[1] // 2
    grads = jnp.sum(gathered[...], axis=0) * (1.0 / total)
    lane = lane_of(grads.shape)

    def prepare(branch):
        if branch == 0:
            state, mean = pltpu.roll(grads, 96, 1), grads[:, 95:96]
        else:
            state, mean = pltpu.roll(grads, 32, 1), grads[:, 31:32]
        state = jnp.where((lane >= 64) & (lane < 96), state, 0.0)
        upper = jnp.where(lane == 96, jnp.broadcast_to(mean, state.shape), state)
        turned = pltpu.roll(jnp.transpose(tall(upper)), 32, 1)
        return jnp.concatenate(halves(turned + tall(state, HEAD)), axis=0)

    def masked(x, query_grad, factor):
        wide = x.astype(F32)
        spot = lane_of(wide.shape)
        left = jnp.where(spot < 64, relu(wide), jnp.where(spot < 96, wide, 1.0)).astype(BF16)
        out = mm(jnp.concatenate([left, left], axis=1), factor)
        keep = ((wide > 0) | (spot >= 64)) & (spot < 96)
        out = jnp.where(keep, out, 0.0).astype(BF16).astype(F32)
        return jnp.where(spot < HEAD, query_grad.astype(F32), out)

    base_factor, side_factor = prepare(0), prepare(1)
    edge = jnp.zeros((MARGIN, span, LANES), F32)
    field[0:MARGIN] = edge
    field[MARGIN + rows : rows + 2 * MARGIN] = edge
    wing = span - cols
    circle = lax.broadcasted_iota(jnp.int32, (wing, LANES), 0)
    shift = jnp.where(circle < 4, circle + cols, circle - wing)
    column = lax.axis_index("col") * cols + shift
    inside = (column >= 0) & (column < lax.axis_size("col") * cols)
    inside = inside & (shift >= -MARGIN) & (shift < cols + MARGIN)
    inside = inside[None]

    def make(i, carry):
        size = 16 * cols
        at = pl.multiple_of(i * size, size)
        out = masked(inner[pl.ds(at, size), :], q_in[1, pl.ds(at, size), :], side_factor)
        field[pl.ds(MARGIN + i * 16, 16), 0:cols] = out.reshape(16, cols, LANES)
        out = masked(base[pl.ds(at, size), :], q_in[0, pl.ds(at, size), :], base_factor)
        straight[pl.ds(i * 16, 16)] = out.reshape(16, cols, LANES)
        size = 16 * wing
        at = pl.multiple_of(i * size, size)
        out = masked(halo[pl.ds(at, size), :], halo_q[pl.ds(at, size), :], side_factor)
        out = jnp.where(inside, out.reshape(16, wing, LANES), 0.0)
        field[pl.ds(MARGIN + i * 16, 16), cols:span] = out
        return carry

    q_move.wait()
    halo_move.wait()
    lax.fori_loop(0, rows // 16, make, 0)
    att_move.wait()
    strip_move.wait()
    proj_move.wait()
    step = 4

    def spread(i, carry):
        block = field[pl.ds(i * step, step + 2 * MARGIN)]
        out = straight[pl.ds(i * step, step)]
        for b in range(TAPS):
            window = pltpu.roll(block, (b - MARGIN) % span, 1)[:, :cols]
            for a in range(TAPS):
                up = 2 * MARGIN - a
                tap = kern[pl.ds(a * TAPS + b, 1), :].reshape(1, 1, LANES)
                out = out + window[up : up + step] * tap
        at = pl.multiple_of(i * step * cols, step * cols)
        size = step * cols
        out = out.reshape(size, LANES)
        out = jnp.where(lane_of(out.shape) < 96, out, att[0, pl.ds(at, size), :].astype(F32))
        tokens_out[pl.ds(at, size), :] = out.astype(BF16)
        return carry

    lax.fori_loop(0, rows // step, spread, 0)

    def taps(i, carry):
        block = strip[pl.ds(i * step, step + 2 * MARGIN)]
        own = field[pl.ds(MARGIN + i * step, step)][:, :cols]
        found = list(carry)
        for b in range(TAPS):
            window = pltpu.roll(block, (MARGIN - b) % span, 1)[:, :cols]
            for a in range(TAPS):
                product = (window[a : a + step] * own).reshape(step * cols // 8, 8, LANES)
                k = a * TAPS + b
                found[k] = found[k] + jnp.sum(product, axis=0)
        return tuple(found)

    zero = jnp.zeros((8, LANES), F32)
    found = lax.fori_loop(0, rows // step, taps, (zero,) * TAPS**2)
    sums[...] = jnp.zeros(sums.shape, F32)
    for k in range(TAPS**2):
        sums[k : k + 1, :] = jnp.sum(found[k], axis=0, keepdims=True)

    def outer(i, carry):
        at = pl.multiple_of(i * 256, 256)
        return carry + mm(tokens_out[pl.ds(at, 256), :], both[pl.ds(at, 256), :channels], (0, 0))

    weight = lax.fori_loop(0, rows * cols // 256, outer, jnp.zeros((LANES, channels), F32))
    parts[0:96] = weight[:96, :LANES]
    parts[96:192] = weight[:96, LANES:]
    parts[192:256] = proj[:, :LANES]
    parts[256:320] = proj[:, LANES:]
    parts[320:352] = sums[...]
    parts[352:384] = jnp.zeros((32, LANES), F32)

    def pack(i, carry):
        at = pl.multiple_of(i * 128, 128)
        x = att[1, pl.ds(at, 128), :].astype(F32)
        out = jnp.zeros((32, LANES), F32)
        spot = lane_of(out.shape)
        for g in range(4):
            turned = pltpu.roll(x[32 * g : 32 * g + 32], (32 * g + 32) % LANES, 1)
            out = jnp.where((spot >= 32 * g) & (spot < 32 * g + 32), turned, out)
        att_out[i] = out.astype(BF16)
        return carry

    lax.fori_loop(0, rows // 8, pack, 0)


def finish_kernel(
    back, tokens_from, grads_from, weights_from, proj_from, block_out, input_out,
    tokens, grads, weights, proj, sems,
):
    heads = back.shape[0]
    moves = [
        move(tokens_from, tokens, sems.at[0]),
        move(grads_from, grads, sems.at[1]),
        move(weights_from, weights, sems.at[2]),
        move(proj_from, proj, sems.at[3]),
    ]
    for copy in moves:
        copy.wait()
    block = tokens[...].astype(F32)
    inputs = grads[...].astype(F32)
    attended = jnp.zeros(block.shape, F32)
    turned = jnp.zeros(block.shape, F32)
    for h in range(heads):
        first = back[h, 0:128, :]
        turned = turned + mm(first, weights[h])
        packed = back[h, 128:160, :].astype(F32)
        side = jnp.concatenate([pltpu.roll(packed, 96 - 32 * g, 1) if g < 3 else packed for g in range(4)], axis=0)
        spot = lane_of(side.shape)
        both = jnp.where(spot >= 96, side, pltpu.roll(first.astype(F32), 96, 1))
        both = jnp.where(spot >= 64, both, 0.0).astype(BF16)
        attended = attended + mm(both, proj[h])
    block_out[...] = (block + attended).astype(BF16)
    input_out[...] = (inputs + turned).astype(BF16)


def assemble_kernel(sums, other, qkv_grad, conv_grad, proj_grad, scratch):
    heads = sums.shape[1]
    core = lax.rem(lax.axis_index("col"), 2)
    for h in range(heads):
        for part in range(sums.shape[0]):
            at = pl.multiple_of(48 * part + 24 * core, 8)
            scratch[h, pl.ds(at, 24), :] = sums[part, h].astype(F32)
            at = pl.multiple_of(48 * part + 24 - 24 * core, 8)
            scratch[h, pl.ds(at, 24), :] = other[part, h].astype(F32)
    for j in range(3):
        for half in range(2):
            for quad in range(heads // 4):
                rows = [
                    scratch[4 * quad + h, 96 * half + 32 * j : 96 * half + 32 * j + 32, :]
                    for h in range(4)
                ]
                block = jnp.transpose(jnp.concatenate(rows, axis=0))
                at = 256 * j + 128 * quad
                qkv_grad[128 * half : 128 * half + 128, at : at + 128] = block
    for j in range(3):
        for quad in range(heads // 4):
            out = jnp.zeros((32, LANES), F32)
            spot = lane_of(out.shape)
            for h in range(4):
                turned = scratch[4 * quad + h, 320:352, :]
                if (h - j) % 4:
                    turned = pltpu.roll(turned, (32 * (h - j)) % LANES, 1)
                out = jnp.where((spot >= 32 * h) & (spot < 32 * h + 32), turned, out)
            at = 256 * j + 128 * quad
            conv_grad[:, at : at + 128] = out[: TAPS**2]
    for h in range(heads):
        for branch in range(2):
            at = 256 * branch + 32 * h
            for half in range(2):
                row = 192 + 64 * half + 32 * branch
                proj_grad[at : at + 32, 128 * half : 128 * half + 128] = scratch[h, row : row + 32, :]


def call(kernel, outs, near, far, scratch=(), sems=0, name=None, keep=True):
    vmem = pl.BlockSpec(memory_space=pltpu.VMEM)
    away = pl.BlockSpec(memory_space=pltpu.HBM)
    shapes, specs = [], []
    for shape, dtype, *flag in outs:
        if flag:
            shapes.append(pltpu.HBM(shape, dtype))
            specs.append(away)
        else:
            held = pltpu.VMEM(shape, dtype) if keep else jax.ShapeDtypeStruct(shape, dtype)
            shapes.append(held)
            specs.append(vmem)
    args = [pltpu.with_memory_space_constraint(arg, pltpu.VMEM) for arg in near]
    scratch = [pltpu.VMEM(shape, dtype) for shape, dtype, *_ in scratch]
    if sems:
        scratch.append(pltpu.SemaphoreType.DMA((sems,)))
    return pl.pallas_call(
        kernel,
        out_shape=shapes,
        in_specs=[vmem] * len(near) + [away] * len(far),
        out_specs=specs,
        scratch_shapes=scratch,
        compiler_params=pltpu.CompilerParams(vmem_limit_bytes=GRANT),
        name=name,
    )(*args, *[pltpu.with_memory_space_constraint(arg, pltpu.HBM) for arg in far])


def exchange(block, axis, groups=None):
    return lax.all_to_all(block, axis, 0, 0, tiled=True, axis_index_groups=groups)


def copies(block, count):
    return jnp.broadcast_to(block[None], (count,) + block.shape)


def local(tokens, qkv_weight, conv_weight, proj_weight, out_grad):
    height, cols, channels = tokens.shape
    heads = lax.axis_size("row")
    strips = lax.axis_size("col")
    head = lax.axis_index("row")
    place = lax.axis_index("col")
    rows = height * heads
    total = float(rows * cols * strips)
    count = rows * cols
    span = cols + 4 * MARGIN

    (spread,) = call(
        spread_kernel,
        [((heads, height, cols, 2 * channels), BF16, "away")],
        [],
        [tokens, out_grad],
        scratch=[((height, cols, 2 * channels), BF16)],
        sems=2 + heads,
        name="spread",
    )
    both = exchange(spread, "row")
    both = both.reshape(count, 2 * channels)

    qkv_heads = qkv_weight.reshape(channels, 3, heads, HEAD).transpose(2, 0, 1, 3)
    qkv_heads = qkv_heads.reshape(heads, channels, 3 * HEAD)
    own_qkv = lax.dynamic_index_in_dim(qkv_heads, head, 0, False)
    own_kernel = conv_weight.reshape(TAPS**2, 3, heads, HEAD)
    own_kernel = lax.dynamic_index_in_dim(own_kernel, head, 2, False).reshape(TAPS**2, 3 * HEAD)
    centre = (jnp.arange(TAPS**2) == TAPS**2 // 2).astype(F32)
    kern = jnp.concatenate(
        [own_kernel.astype(F32), jnp.broadcast_to(centre[:, None], (TAPS**2, HEAD))], axis=1
    )
    proj_heads = proj_weight.reshape(2, heads, HEAD, channels).transpose(1, 0, 2, 3)
    proj_heads = proj_heads.reshape(heads, 2 * HEAD, channels)
    own_proj = lax.dynamic_index_in_dim(proj_heads, head, 0, False)
    blank = jnp.zeros((channels, HEAD), BF16)
    blanks = jnp.zeros((channels, 3 * HEAD), BF16)
    upper = jnp.concatenate([own_qkv, blank], axis=1)
    side_map = jnp.concatenate([upper, jnp.concatenate([blanks, own_proj[HEAD:].T], axis=1)])
    base_map = jnp.concatenate([upper, jnp.concatenate([blanks, own_proj[:HEAD].T], axis=1)])
    sent = mm(both, side_map).astype(BF16).reshape(rows, cols, LANES)
    base = mm(both, base_map).astype(BF16)

    even = place % 2 == 0
    first, last = sent[:, :4], sent[:, cols - 4 :]
    apart = [(i, i + 1) for i in range(1, strips - 1, 2)]
    apart += [(j, i) for i, j in apart]
    beside = [(i, i ^ 1) for i in range(strips)]
    far = lax.ppermute(jnp.where(even, first, last), "col", apart)
    near = lax.ppermute(jnp.where(even, last, first), "col", beside)

    wings = rows * (span - cols)
    small = (strips, HEAD, LANES)
    tall_strip = ((rows + 2 * MARGIN, span, LANES), F32, "away")
    inner, halo, strip, pack = call(
        aggregate_kernel,
        [((count, LANES), BF16), ((wings, LANES), BF16), tall_strip, (small, F32)],
        [sent, near, far, base, kern],
        [],
        scratch=[tall_strip],
        sems=1,
        name="aggregate",
    )
    gathered = exchange(pack, "col")
    terms = [
        ((2, count, LANES), F32, "away"),
        ((2, count, LANES), BF16, "away"),
        ((2, HEAD, LANES), F32, "away"),
        ((2 * LANES, 2 * LANES), BF16, "away"),
    ]
    y, att, maps, factor, pack = call(
        lambda *refs: forward_kernel(total, *refs),
        terms + [(small, F32, "away")],
        [gathered, base, inner],
        [],
        scratch=terms + [((HEAD, LANES), F32)],
        sems=6 + strips,
        name="forward",
    )
    gathered = exchange(pack, "col")
    parts = [
        ((2, count, LANES), BF16, "away"),
        ((wings, LANES), BF16, "away"),
        ((2 * HEAD, channels), F32, "away"),
    ]
    q, halo_q, proj = call(
        query_kernel,
        parts,
        [base, inner, halo, both],
        [y, maps, factor, att],
        scratch=[terms[0], terms[2], terms[3], terms[1]] + parts,
        sems=4,
        name="query",
    )
    tokens_out, att_out, parts = call(
        lambda *refs: backward_kernel(total, *refs),
        [((count, LANES), BF16), ((heads, 32, LANES), BF16), ((384, LANES), F32)],
        [gathered, base, inner, halo, kern, both],
        [q, halo_q, att, strip, proj],
        scratch=[
            parts[0],
            parts[1],
            terms[1],
            tall_strip,
            parts[2],
            tall_strip,
            ((rows, cols, LANES), F32),
            ((32, LANES), F32),
        ],
        sems=5,
        name="backward",
    )
    part = exchange(parts.reshape(strips, 24, LANES), "col")
    part = jnp.sum(part, axis=0).astype(BF16)
    sent_back = jnp.concatenate(
        [tokens_out.reshape(heads, -1, LANES), att_out, copies(part, heads)], axis=1
    )
    back = exchange(sent_back, "row")
    sums = back[:, 160:]
    groups = [[2 * i + c for i in range(strips // 2)] for c in range(2)]
    sums = exchange(copies(sums, strips // 2), "col", groups)
    other = lax.ppermute(sums, "col", beside)

    weights = jnp.pad(qkv_heads.transpose(0, 2, 1), ((0, 0), (0, HEAD), (0, 0)))
    proj_rows = jnp.pad(proj_heads, ((0, 0), (2 * HEAD, 0), (0, 0)))
    block_output, input_grad = call(
        finish_kernel,
        [((height * cols, channels), BF16)] * 2,
        [back],
        [tokens.reshape(-1, channels), out_grad.reshape(-1, channels), weights, proj_rows],
        scratch=[
            ((height * cols, channels), BF16),
            ((height * cols, channels), BF16),
            ((heads, LANES, channels), BF16),
            ((heads, LANES, channels), BF16),
        ],
        sems=4,
        name="finish",
        keep=False,
    )
    qkv_grad, conv_grad, proj_grad = call(
        assemble_kernel,
        [
            ((channels, 3 * channels), F32),
            ((TAPS**2, 3 * channels), F32),
            ((2 * channels, channels), F32),
        ],
        [sums, other],
        [],
        scratch=[((heads, 384, LANES), F32)],
        name="assemble",
        keep=False,
    )
    return (
        block_output.reshape(tokens.shape),
        input_grad.reshape(tokens.shape),
        qkv_grad,
        conv_grad,
        proj_grad,
    )


def solution(mesh):
    placed = (P("row", "col", None), P(), P(), P(), P("row", "col", None))
    return jax.shard_map(
        local,
        mesh=mesh,
        in_specs=placed,
        out_specs=(P("row", "col", None), P("row", "col", None), P(), P(), P()),
        check_vma=False,
    )
```

```python
import jax
import jax.numpy as jnp
from jax import lax
from jax.experimental import pallas as pl
from jax.experimental.pallas import tpu as pltpu
from jax.sharding import PartitionSpec as P

HEAD = 32
TAPS = 5
MARGIN = TAPS // 2
LANES = 4 * HEAD
GRANT = 16 * 2**20

F32 = jnp.float32
BF16 = jnp.bfloat16


def lane_of(shape):
    return lax.broadcasted_iota(jnp.int32, shape, len(shape) - 1)


def halves(x):
    high = x.astype(BF16)
    return high, (x - high.astype(F32)).astype(BF16)


def mm(left, right, contract=(1, 0)):
    dims = (((contract[0],), (contract[1],)), ((), ()))
    return lax.dot_general(left, right, dims, preferred_element_type=F32)


def relu(x):
    return jnp.maximum(x, jnp.zeros((), x.dtype))


def pair_up(base, side):
    lane = lane_of(base.shape)
    return jnp.where(lane < 64, pltpu.roll(side, 64, 1), base)


def tall(matrix, above=0):
    below = LANES - HEAD - above
    parts = [jnp.zeros((above, matrix.shape[1]), F32)] if above else []
    parts += [matrix, jnp.zeros((below, matrix.shape[1]), F32)]
    return jnp.concatenate(parts, axis=0)


def move(source, target, sem):
    copy = pltpu.make_async_copy(source, target, sem)
    copy.start()
    return copy


def spread_kernel(tokens, grads, out, buffer, sems):
    channels = tokens.shape[2]
    first = move(tokens, buffer.at[:, :, 0:channels], sems.at[0])
    second = move(grads, buffer.at[:, :, channels : 2 * channels], sems.at[1])
    first.wait()
    second.wait()
    moves = [move(buffer, out.at[i], sems.at[2 + i]) for i in range(out.shape[0])]
    for copy in moves:
        copy.wait()


def aggregate_kernel(sent, near, far, base, kern, inner, halo, strip_out, pack, strip, sems):
    rows, cols, _ = sent.shape
    span = strip.shape[1]
    even = lax.rem(lax.axis_index("col"), 2) == 0
    low = jnp.where(even, far[...].astype(F32), near[...].astype(F32))
    high = jnp.where(even, near[...].astype(F32), far[...].astype(F32))
    edge = jnp.zeros((MARGIN, span, LANES), F32)
    strip[0:MARGIN] = edge
    strip[MARGIN + rows : rows + 2 * MARGIN] = edge
    strip[MARGIN : MARGIN + rows, 0:cols] = sent[...].astype(F32)
    strip[MARGIN : MARGIN + rows, cols : cols + 4] = high
    strip[MARGIN : MARGIN + rows, cols + 4 : cols + 8] = low
    strip_move = move(strip, strip_out, sems.at[0])
    step = 4

    def conv(i, carry):
        block = strip[pl.ds(i * step, step + 2 * MARGIN)]
        total = jnp.zeros((step, span, LANES), F32)
        for b in range(TAPS):
            window = pltpu.roll(block, (MARGIN - b) % span, 1)
            for a in range(TAPS):
                tap = kern[pl.ds(a * TAPS + b, 1), :].reshape(1, 1, LANES)
                total = total + window[a : a + step] * tap
        size = step * cols
        at = pl.multiple_of(i * size, size)
        inner[pl.ds(at, size), :] = total[:, :cols].reshape(size, LANES).astype(BF16)
        size = step * (span - cols)
        at = pl.multiple_of(i * size, size)
        halo[pl.ds(at, size), :] = total[:, cols:].reshape(size, LANES).astype(BF16)
        return carry

    lax.fori_loop(0, rows // step, conv, 0)

    def outer(x):
        ones = jnp.where(lane_of(x.shape) >= 96, jnp.ones((), BF16), x)
        return mm(relu(x), ones, (0, 0))[HEAD : 2 * HEAD]

    def states(i, carry):
        at = pl.multiple_of(i * 256, 256)
        base_sum = carry[0] + outer(base[pl.ds(at, 256), :])
        side_sum = carry[1] + outer(inner[pl.ds(at, 256), :])
        return base_sum, side_sum

    zero = jnp.zeros((HEAD, LANES), F32)
    base_sum, side_sum = lax.fori_loop(0, rows * cols // 256, states, (zero, zero))
    both_sums = pair_up(base_sum, side_sum).astype(BF16)
    pack[...] = jnp.broadcast_to(both_sums[None], pack.shape)
    strip_move.wait()


def token_terms(x, factor):
    query = relu(x)
    wide = x.astype(F32)
    spot = lane_of(wide.shape)
    products = mm(jnp.concatenate([query, query], axis=1), factor)
    numerator = products[:, :LANES]
    inverse = 1.0 / (products[:, LANES:] + 1.0)
    along = jnp.sum(jnp.where(spot >= 96, wide * numerator, 0.0), axis=1, keepdims=True)
    y = jnp.where(spot >= 96, wide * inverse, 0.0)
    y = jnp.where(spot == 95, -along * inverse * inverse, y)
    return query, numerator * inverse, y


def forward_kernel(total, gathered, base, inner, maps_out, factor_out, pack_out, maps, factor, pack, sems):
    states = jnp.sum(gathered[...].astype(F32), axis=0) * (1.0 / total)
    lane = lane_of(states.shape)
    for branch in range(2):
        if branch == 0:
            state, mean = pltpu.roll(states, 32, 1), states[:, 96:97]
        else:
            state, mean = pltpu.roll(states, 96, 1), states[:, 32:33]
        mean = jnp.broadcast_to(mean, states.shape)
        state = jnp.where(lane >= 96, state, 0.0)
        maps[branch] = jnp.where(lane == 95, mean, state)
        parts = halves(tall(jnp.concatenate([state, mean], axis=1)))
        factor[branch] = jnp.concatenate(parts, axis=0)
    moves = [move(maps, maps_out, sems.at[0]), move(factor, factor_out, sems.at[1])]

    factors = (factor[0], factor[1])

    def step(i, carry):
        at = pl.multiple_of(i * 256, 256)
        found = []
        for branch, ref in enumerate((base, inner)):
            query, _, own = token_terms(ref[pl.ds(at, 256), :], factors[branch])
            both_halves = jnp.concatenate(halves(own), axis=1)
            found.append(carry[branch] + mm(query, both_halves, (0, 0))[:HEAD])
        return tuple(found)

    zero = jnp.zeros((HEAD, 2 * LANES), F32)
    found = lax.fori_loop(0, base.shape[0] // 256, step, (zero, zero))
    found = [pair[:, :LANES] + pair[:, LANES:] for pair in found]
    pack[...] = jnp.broadcast_to(pair_up(*found).astype(BF16)[None], pack.shape)
    moves.append(move(pack, pack_out, sems.at[2]))
    for copy in moves:
        copy.wait()


def query_kernel(
    base, inner, halo, both, maps_in, factor_in, q_out, att_out, halo_out, proj_out,
    maps, factor, q, att, halo_q, proj, sems,
):
    channels = both.shape[1] // 2
    first, second = move(maps_in, maps, sems.at[0]), move(factor_in, factor, sems.at[1])
    first.wait()
    second.wait()

    def query_grad(x, y, parts):
        high, low = halves(y)
        out = mm(jnp.concatenate([high, low], axis=1), parts[0], (1, 1)) + mm(high, parts[1], (1, 1))
        return jnp.where(x.astype(F32) > 0, out, 0.0).astype(BF16)

    moves = []
    for branch, ref in enumerate((base, inner)):
        high, low = halves(tall(maps[branch]))
        parts = (jnp.concatenate([high, high], axis=1), low)
        factors = factor[branch]

        def step(i, carry):
            at = pl.multiple_of(i * 256, 256)
            x = ref[pl.ds(at, 256), :]
            _, out, y = token_terms(x, factors)
            out = out.astype(BF16)
            att[branch, pl.ds(at, 256), :] = out
            q[branch, pl.ds(at, 256), :] = query_grad(x, y, parts)
            grads = both[pl.ds(at, 256), channels:]
            return carry + mm(out, grads, (0, 0))[96:]

        zero = jnp.zeros((HEAD, channels), F32)
        found = lax.fori_loop(0, ref.shape[0] // 256, step, zero)
        proj[HEAD * branch : HEAD * branch + HEAD] = found
        moves.append(move(q.at[branch], q_out.at[branch], sems.at[2 + branch]))
        moves.append(move(att.at[branch], att_out.at[branch], sems.at[4 + branch]))

    def edge(i, carry):
        at = pl.multiple_of(i * 256, 256)
        x = halo[pl.ds(at, 256), :]
        halo_q[pl.ds(at, 256), :] = query_grad(x, token_terms(x, factors)[2], parts)
        return carry

    lax.fori_loop(0, halo.shape[0] // 256, edge, 0)
    moves += [move(halo_q, halo_out, sems.at[6]), move(proj, proj_out, sems.at[7])]
    for copy in moves:
        copy.wait()


def backward_kernel(
    total, gathered, base, inner, halo, kern, both, q_from, halo_from, att_from, strip_from, proj_from,
    tokens_out, att_out, parts, q_in, halo_q, att, strip, proj, field, straight, sums, sems,
):
    q_move = move(q_from, q_in, sems.at[0])
    halo_move = move(halo_from, halo_q, sems.at[1])
    att_move = move(att_from, att, sems.at[2])
    strip_move = move(strip_from, strip, sems.at[3])
    proj_move = move(proj_from, proj, sems.at[4])
    span = strip.shape[1]
    rows = strip.shape[0] - 2 * MARGIN
    cols = base.shape[0] // rows
    channels = both.shape[1] // 2
    grads = jnp.sum(gathered[...].astype(F32), axis=0) * (1.0 / total)
    lane = lane_of(grads.shape)

    def prepare(branch):
        if branch == 0:
            state, mean = pltpu.roll(grads, 96, 1), grads[:, 95:96]
        else:
            state, mean = pltpu.roll(grads, 32, 1), grads[:, 31:32]
        state = jnp.where((lane >= 64) & (lane < 96), state, 0.0)
        upper = jnp.where(lane == 96, jnp.broadcast_to(mean, state.shape), state)
        turned = pltpu.roll(jnp.transpose(tall(upper)), 32, 1)
        return jnp.concatenate(halves(turned + tall(state, HEAD)), axis=0)

    def masked(x, query_grad, factor):
        wide = x.astype(F32)
        spot = lane_of(wide.shape)
        left = jnp.where(spot < 64, relu(wide), jnp.where(spot < 96, wide, 1.0)).astype(BF16)
        out = mm(jnp.concatenate([left, left], axis=1), factor)
        keep = ((wide > 0) | (spot >= 64)) & (spot < 96)
        out = jnp.where(keep, out, 0.0).astype(BF16).astype(F32)
        return jnp.where(spot < HEAD, query_grad.astype(F32), out)

    base_factor, side_factor = prepare(0), prepare(1)
    edge = jnp.zeros((MARGIN, span, LANES), F32)
    field[0:MARGIN] = edge
    field[MARGIN + rows : rows + 2 * MARGIN] = edge
    wing = span - cols
    circle = lax.broadcasted_iota(jnp.int32, (wing, LANES), 0)
    shift = jnp.where(circle < 4, circle + cols, circle - wing)
    column = lax.axis_index("col") * cols + shift
    inside = (column >= 0) & (column < lax.axis_size("col") * cols)
    inside = inside & (shift >= -MARGIN) & (shift < cols + MARGIN)
    inside = inside[None]

    def make(i, carry):
        size = 16 * cols
        at = pl.multiple_of(i * size, size)
        out = masked(inner[pl.ds(at, size), :], q_in[1, pl.ds(at, size), :], side_factor)
        field[pl.ds(MARGIN + i * 16, 16), 0:cols] = out.reshape(16, cols, LANES)
        out = masked(base[pl.ds(at, size), :], q_in[0, pl.ds(at, size), :], base_factor)
        straight[pl.ds(i * 16, 16)] = out.reshape(16, cols, LANES)
        size = 16 * wing
        at = pl.multiple_of(i * size, size)
        out = masked(halo[pl.ds(at, size), :], halo_q[pl.ds(at, size), :], side_factor)
        out = jnp.where(inside, out.reshape(16, wing, LANES), 0.0)
        field[pl.ds(MARGIN + i * 16, 16), cols:span] = out
        return carry

    q_move.wait()
    halo_move.wait()
    lax.fori_loop(0, rows // 16, make, 0)
    att_move.wait()
    strip_move.wait()
    proj_move.wait()
    step = 4

    def spread(i, carry):
        step = 8
        block = field[pl.ds(i * step, step + 2 * MARGIN)]
        out = straight[pl.ds(i * step, step)]
        for b in range(TAPS):
            window = pltpu.roll(block, (b - MARGIN) % span, 1)[:, :cols]
            for a in range(TAPS):
                up = 2 * MARGIN - a
                tap = kern[pl.ds(a * TAPS + b, 1), :].reshape(1, 1, LANES)
                out = out + window[up : up + step] * tap
        at = pl.multiple_of(i * step * cols, step * cols)
        size = step * cols
        out = out.reshape(size, LANES)
        out = jnp.where(lane_of(out.shape) < 96, out, att[0, pl.ds(at, size), :].astype(F32))
        tokens_out[pl.ds(at, size), :] = out.astype(BF16)
        return carry

    lax.fori_loop(0, rows // 8, spread, 0)

    def taps(i, carry):
        block = strip[pl.ds(i * step, step + 2 * MARGIN)]
        own = field[pl.ds(MARGIN + i * step, step)][:, :cols]
        found = list(carry)
        for b in range(TAPS):
            window = pltpu.roll(block, (MARGIN - b) % span, 1)[:, :cols]
            for a in range(TAPS):
                product = (window[a : a + step] * own).reshape(step * cols // 8, 8, LANES)
                k = a * TAPS + b
                found[k] = found[k] + jnp.sum(product, axis=0)
        return tuple(found)

    zero = jnp.zeros((8, LANES), F32)
    found = lax.fori_loop(0, rows // step, taps, (zero,) * TAPS**2)
    sums[...] = jnp.zeros(sums.shape, F32)
    for k in range(TAPS**2):
        sums[k : k + 1, :] = jnp.sum(found[k], axis=0, keepdims=True)

    def outer(i, carry):
        at = pl.multiple_of(i * 256, 256)
        return carry + mm(tokens_out[pl.ds(at, 256), :], both[pl.ds(at, 256), :channels], (0, 0))

    weight = lax.fori_loop(0, rows * cols // 256, outer, jnp.zeros((LANES, channels), F32))
    parts[0:96] = weight[:96, :LANES].astype(BF16)
    parts[96:192] = weight[:96, LANES:].astype(BF16)
    parts[192:256] = proj[:, :LANES].astype(BF16)
    parts[256:320] = proj[:, LANES:].astype(BF16)
    parts[320:352] = sums[...].astype(BF16)
    parts[352:384] = jnp.zeros((32, LANES), BF16)

    def pack(i, carry):
        at = pl.multiple_of(i * 128, 128)
        x = att[1, pl.ds(at, 128), :].astype(F32)
        out = jnp.zeros((32, LANES), F32)
        spot = lane_of(out.shape)
        for g in range(4):
            turned = pltpu.roll(x[32 * g : 32 * g + 32], (32 * g + 32) % LANES, 1)
            out = jnp.where((spot >= 32 * g) & (spot < 32 * g + 32), turned, out)
        att_out[i] = out.astype(BF16)
        return carry

    lax.fori_loop(0, rows // 8, pack, 0)


def finish_kernel(
    back, tokens_from, grads_from, weights_from, proj_from, block_out, input_out,
    tokens, grads, weights, proj, sems,
):
    heads = back.shape[0]
    blank = jnp.zeros((heads, HEAD, weights.shape[2]), BF16)
    weights[:, 3 * HEAD :] = blank
    proj[:, :HEAD] = blank
    proj[:, HEAD : 2 * HEAD] = blank
    moves = [
        move(tokens_from, tokens, sems.at[0]),
        move(grads_from, grads, sems.at[1]),
        move(weights_from, weights.at[:, 0 : 3 * HEAD], sems.at[2]),
        move(proj_from, proj.at[:, 2 * HEAD : LANES], sems.at[3]),
    ]
    mixed = []
    for h in range(heads):
        first = back[h, 0:128, :]
        packed = back[h, 128:160, :].astype(F32)
        side = jnp.concatenate([pltpu.roll(packed, 96 - 32 * g, 1) if g < 3 else packed for g in range(4)], axis=0)
        spot = lane_of(side.shape)
        both = jnp.where(spot >= 96, side, pltpu.roll(first.astype(F32), 96, 1))
        mixed.append(jnp.where(spot >= 64, both, 0.0).astype(BF16))
    for copy in moves:
        copy.wait()
    attended = jnp.zeros(tokens.shape, F32)
    turned = jnp.zeros(tokens.shape, F32)
    for h in range(heads):
        turned = turned + mm(back[h, 0:128, :], weights[h])
        attended = attended + mm(mixed[h], proj[h])
    block_out[...] = (tokens[...].astype(F32) + attended).astype(BF16)
    input_out[...] = (grads[...].astype(F32) + turned).astype(BF16)


def assemble_kernel(sums, other, qkv_grad, conv_grad, proj_grad, scratch):
    heads = sums.shape[1]
    core = lax.rem(lax.axis_index("col"), 2)
    for h in range(heads):
        for part in range(sums.shape[0]):
            at = pl.multiple_of(48 * part + 24 * core, 8)
            scratch[h, pl.ds(at, 24), :] = sums[part, h].astype(F32)
            at = pl.multiple_of(48 * part + 24 - 24 * core, 8)
            scratch[h, pl.ds(at, 24), :] = other[part, h].astype(F32)
    for j in range(3):
        for half in range(2):
            for quad in range(heads // 4):
                rows = [
                    scratch[4 * quad + h, 96 * half + 32 * j : 96 * half + 32 * j + 32, :]
                    for h in range(4)
                ]
                block = jnp.transpose(jnp.concatenate(rows, axis=0))
                at = 256 * j + 128 * quad
                qkv_grad[128 * half : 128 * half + 128, at : at + 128] = block
    for j in range(3):
        for quad in range(heads // 4):
            out = jnp.zeros((32, LANES), F32)
            spot = lane_of(out.shape)
            for h in range(4):
                turned = scratch[4 * quad + h, 320:352, :]
                if (h - j) % 4:
                    turned = pltpu.roll(turned, (32 * (h - j)) % LANES, 1)
                out = jnp.where((spot >= 32 * h) & (spot < 32 * h + 32), turned, out)
            at = 256 * j + 128 * quad
            conv_grad[:, at : at + 128] = out[: TAPS**2]
    for h in range(heads):
        for branch in range(2):
            at = 256 * branch + 32 * h
            for half in range(2):
                row = 192 + 64 * half + 32 * branch
                proj_grad[at : at + 32, 128 * half : 128 * half + 128] = scratch[h, row : row + 32, :]


def call(kernel, outs, near, far, scratch=(), sems=0, name=None, keep=True):
    vmem = pl.BlockSpec(memory_space=pltpu.VMEM)
    away = pl.BlockSpec(memory_space=pltpu.HBM)
    shapes, specs = [], []
    for shape, dtype, *flag in outs:
        if flag:
            shapes.append(pltpu.HBM(shape, dtype))
            specs.append(away)
        else:
            held = pltpu.VMEM(shape, dtype) if keep else jax.ShapeDtypeStruct(shape, dtype)
            shapes.append(held)
            specs.append(vmem)
    args = [pltpu.with_memory_space_constraint(arg, pltpu.VMEM) for arg in near]
    scratch = [pltpu.VMEM(shape, dtype) for shape, dtype, *_ in scratch]
    if sems:
        scratch.append(pltpu.SemaphoreType.DMA((sems,)))
    return pl.pallas_call(
        kernel,
        out_shape=shapes,
        in_specs=[vmem] * len(near) + [away] * len(far),
        out_specs=specs,
        scratch_shapes=scratch,
        compiler_params=pltpu.CompilerParams(vmem_limit_bytes=GRANT),
        name=name,
    )(*args, *[pltpu.with_memory_space_constraint(arg, pltpu.HBM) for arg in far])


def exchange(block, axis, groups=None):
    return lax.all_to_all(block, axis, 0, 0, tiled=True, axis_index_groups=groups)


def copies(block, count):
    return jnp.broadcast_to(block[None], (count,) + block.shape)


def local(tokens, qkv_weight, conv_weight, proj_weight, out_grad):
    height, cols, channels = tokens.shape
    heads = lax.axis_size("row")
    strips = lax.axis_size("col")
    head = lax.axis_index("row")
    place = lax.axis_index("col")
    rows = height * heads
    total = float(rows * cols * strips)
    count = rows * cols
    span = cols + 4 * MARGIN

    (spread,) = call(
        spread_kernel,
        [((heads, height, cols, 2 * channels), BF16, "away")],
        [],
        [tokens, out_grad],
        scratch=[((height, cols, 2 * channels), BF16)],
        sems=2 + heads,
        name="spread",
    )
    both = exchange(spread, "row")
    both = both.reshape(count, 2 * channels)

    qkv_heads = qkv_weight.reshape(channels, 3, heads, HEAD).transpose(2, 0, 1, 3)
    qkv_heads = qkv_heads.reshape(heads, channels, 3 * HEAD)
    own_qkv = lax.dynamic_index_in_dim(qkv_heads, head, 0, False)
    own_kernel = conv_weight.reshape(TAPS**2, 3, heads, HEAD)
    own_kernel = lax.dynamic_index_in_dim(own_kernel, head, 2, False).reshape(TAPS**2, 3 * HEAD)
    centre = (jnp.arange(TAPS**2) == TAPS**2 // 2).astype(F32)
    kern = jnp.concatenate(
        [own_kernel.astype(F32), jnp.broadcast_to(centre[:, None], (TAPS**2, HEAD))], axis=1
    )
    proj_heads = proj_weight.reshape(2, heads, HEAD, channels).transpose(1, 0, 2, 3)
    proj_heads = proj_heads.reshape(heads, 2 * HEAD, channels)
    own_proj = lax.dynamic_index_in_dim(proj_heads, head, 0, False)
    blank = jnp.zeros((channels, HEAD), BF16)
    blanks = jnp.zeros((channels, 3 * HEAD), BF16)
    upper = jnp.concatenate([own_qkv, blank], axis=1)
    side_map = jnp.concatenate([upper, jnp.concatenate([blanks, own_proj[HEAD:].T], axis=1)])
    base_map = jnp.concatenate([upper, jnp.concatenate([blanks, own_proj[:HEAD].T], axis=1)])
    sent = mm(both, side_map).astype(BF16).reshape(rows, cols, LANES)
    base = mm(both, base_map).astype(BF16)

    even = place % 2 == 0
    first, last = sent[:, :4], sent[:, cols - 4 :]
    apart = [(i, i + 1) for i in range(1, strips - 1, 2)]
    apart += [(j, i) for i, j in apart]
    beside = [(i, i ^ 1) for i in range(strips)]
    far = lax.ppermute(jnp.where(even, first, last), "col", apart)
    near = lax.ppermute(jnp.where(even, last, first), "col", beside)

    wings = rows * (span - cols)
    small = (strips, HEAD, LANES)
    tall_strip = ((rows + 2 * MARGIN, span, LANES), F32, "away")
    inner, halo, strip, pack = call(
        aggregate_kernel,
        [((count, LANES), BF16), ((wings, LANES), BF16), tall_strip, (small, BF16)],
        [sent, near, far, base, kern],
        [],
        scratch=[tall_strip],
        sems=1,
        name="aggregate",
    )
    gathered = exchange(pack, "col")
    terms = [((2, HEAD, LANES), F32, "away"), ((2, 2 * LANES, 2 * LANES), BF16, "away")]
    maps, factor, pack = call(
        lambda *refs: forward_kernel(total, *refs),
        terms + [(small, BF16, "away")],
        [gathered, base, inner],
        [],
        scratch=terms + [(small, BF16)],
        sems=3,
        name="forward",
    )
    gathered = exchange(pack, "col")
    tokens_shape = ((2, count, LANES), BF16, "away")
    parts = [
        tokens_shape,
        tokens_shape,
        ((wings, LANES), BF16, "away"),
        ((2 * HEAD, channels), F32, "away"),
    ]
    q, att, halo_q, proj = call(
        query_kernel,
        parts,
        [base, inner, halo, both],
        [maps, factor],
        scratch=terms + parts,
        sems=8,
        name="query",
    )
    tokens_out, att_out, parts = call(
        lambda *refs: backward_kernel(total, *refs),
        [((count, LANES), BF16), ((heads, 32, LANES), BF16), ((384, LANES), BF16)],
        [gathered, base, inner, halo, kern, both],
        [q, halo_q, att, strip, proj],
        scratch=[
            tokens_shape,
            parts[2],
            tokens_shape,
            tall_strip,
            parts[3],
            tall_strip,
            ((rows, cols, LANES), F32),
            ((32, LANES), F32),
        ],
        sems=5,
        name="backward",
    )
    part = exchange(parts.reshape(strips, 24, LANES), "col")
    part = jnp.sum(part.astype(F32), axis=0).astype(BF16)
    sent_back = jnp.concatenate(
        [tokens_out.reshape(heads, -1, LANES), att_out, copies(part, heads)], axis=1
    )
    back = exchange(sent_back, "row")
    sums = back[:, 160:]
    groups = [[2 * i + c for i in range(strips // 2)] for c in range(2)]
    sums = exchange(copies(sums, strips // 2), "col", groups)
    weights = qkv_heads.transpose(0, 2, 1)
    block_output, input_grad = call(
        finish_kernel,
        [((height * cols, channels), BF16)] * 2,
        [back],
        [tokens.reshape(-1, channels), out_grad.reshape(-1, channels), weights, proj_heads],
        scratch=[
            ((height * cols, channels), BF16),
            ((height * cols, channels), BF16),
            ((heads, LANES, channels), BF16),
            ((heads, LANES, channels), BF16),
        ],
        sems=4,
        name="finish",
        keep=False,
    )
    other = lax.ppermute(sums, "col", beside)
    qkv_grad, conv_grad, proj_grad = call(
        assemble_kernel,
        [
            ((channels, 3 * channels), F32),
            ((TAPS**2, 3 * channels), F32),
            ((2 * channels, channels), F32),
        ],
        [sums, other],
        [],
        scratch=[((heads, 384, LANES), F32)],
        name="assemble",
        keep=False,
    )
    return (
        block_output.reshape(tokens.shape),
        input_grad.reshape(tokens.shape),
        qkv_grad,
        conv_grad,
        proj_grad,
    )


def solution(mesh):
    placed = (P("row", "col", None), P(), P(), P(), P("row", "col", None))
    return jax.shard_map(
        local,
        mesh=mesh,
        in_specs=placed,
        out_specs=(P("row", "col", None), P("row", "col", None), P(), P(), P()),
        check_vma=False,
    )
```

```python
import jax
import jax.numpy as jnp
from jax import lax
from jax.experimental import pallas as pl
from jax.experimental.pallas import tpu as pltpu
from jax.sharding import PartitionSpec as P

HEAD = 32
TAPS = 5
MARGIN = TAPS // 2
LANES = 4 * HEAD
WING = 4 * MARGIN
GRANT = 16 * 2**20

F32 = jnp.float32
BF16 = jnp.bfloat16


def lane_of(shape):
    return lax.broadcasted_iota(jnp.int32, shape, len(shape) - 1)


def halves(x):
    high = x.astype(BF16)
    return high, (x - high.astype(F32)).astype(BF16)


def mm(left, right, contract=(1, 0)):
    dims = (((contract[0],), (contract[1],)), ((), ()))
    return lax.dot_general(left, right, dims, preferred_element_type=F32)


def relu(x):
    return jnp.maximum(x, jnp.zeros((), x.dtype))


def pair_up(base, side):
    lane = lane_of(base.shape)
    return jnp.where(lane < 64, pltpu.roll(side, 64, 1), base)


def tall(matrix, above=0):
    below = LANES - HEAD - above
    parts = [jnp.zeros((above, matrix.shape[1]), F32)] if above else []
    parts += [matrix, jnp.zeros((below, matrix.shape[1]), F32)]
    return jnp.concatenate(parts, axis=0)


def move(source, target, sem):
    copy = pltpu.make_async_copy(source, target, sem)
    copy.start()
    return copy


def spread_kernel(tokens, grads, out, buffer, sems):
    channels = tokens.shape[2]
    first = move(tokens, buffer.at[:, :, 0:channels], sems.at[0])
    second = move(grads, buffer.at[:, :, channels : 2 * channels], sems.at[1])
    first.wait()
    second.wait()
    moves = [move(buffer, out.at[i], sems.at[2 + i]) for i in range(out.shape[0])]
    for copy in moves:
        copy.wait()


def aggregate_kernel(sent, near, far, base, kern, inner, halo, strip_out, pack, strip, sems):
    rows, cols, _ = sent.shape
    span = cols + WING
    even = lax.rem(lax.axis_index("col"), 2) == 0
    low = jnp.where(even, far[...].astype(F32), near[...].astype(F32))
    high = jnp.where(even, near[...].astype(F32), far[...].astype(F32))
    edge = jnp.zeros((MARGIN,) + strip.shape[1:], F32)
    strip[0:MARGIN] = edge
    strip[MARGIN + rows : rows + 2 * MARGIN] = edge
    strip[MARGIN : MARGIN + rows, WING : WING + cols] = sent[...].astype(F32)
    strip[MARGIN : MARGIN + rows, WING + span : 2 * WING + span] = sent[:, :WING].astype(F32)
    for at in (0, span):
        strip[MARGIN : MARGIN + rows, at : at + 4] = high
        strip[MARGIN : MARGIN + rows, at + 4 : at + 8] = low
    strip_move = move(strip.at[:, 0 : span + WING], strip_out, sems.at[0])
    step = 4

    def conv(i, carry):
        total = jnp.zeros((step, span, LANES), F32)
        for b in range(TAPS):
            at = WING - MARGIN + b
            for a in range(TAPS):
                tap = kern[pl.ds(a * TAPS + b, 1), :].reshape(1, 1, LANES)
                total = total + strip[pl.ds(i * step + a, step), at : at + span] * tap
        size = step * cols
        at = pl.multiple_of(i * size, size)
        inner[pl.ds(at, size), :] = total[:, :cols].reshape(size, LANES).astype(BF16)
        size = step * (span - cols)
        at = pl.multiple_of(i * size, size)
        halo[pl.ds(at, size), :] = total[:, cols:].reshape(size, LANES).astype(BF16)
        return carry

    lax.fori_loop(0, rows // step, conv, 0)

    def outer(x):
        ones = jnp.where(lane_of(x.shape) >= 96, jnp.ones((), BF16), x)
        return mm(relu(x), ones, (0, 0))[HEAD : 2 * HEAD]

    def states(i, carry):
        at = pl.multiple_of(i * 1024, 1024)
        base_sum = carry[0] + outer(base[pl.ds(at, 1024), :])
        side_sum = carry[1] + outer(inner[pl.ds(at, 1024), :])
        return base_sum, side_sum

    zero = jnp.zeros((HEAD, LANES), F32)
    base_sum, side_sum = lax.fori_loop(0, rows * cols // 1024, states, (zero, zero))
    both_sums = pair_up(base_sum, side_sum).astype(BF16)
    pack[...] = jnp.broadcast_to(both_sums[None], pack.shape)
    strip_move.wait()


def token_terms(x, factor):
    query = relu(x)
    wide = x.astype(F32)
    spot = lane_of(wide.shape)
    products = mm(jnp.concatenate([query, query], axis=1), factor)
    numerator = products[:, :LANES]
    inverse = 1.0 / (products[:, LANES:] + 1.0)
    along = jnp.sum(jnp.where(spot >= 96, wide * numerator, 0.0), axis=1, keepdims=True)
    y = jnp.where(spot >= 96, wide * inverse, 0.0)
    y = jnp.where(spot == 95, -along * inverse * inverse, y)
    return query, numerator * inverse, y


def forward_kernel(total, gathered, base, inner, maps_out, factor_out, pack_out, maps, factor, pack, sems):
    states = jnp.sum(gathered[...].astype(F32), axis=0) * (1.0 / total)
    lane = lane_of(states.shape)
    for branch in range(2):
        if branch == 0:
            state, mean = pltpu.roll(states, 32, 1), states[:, 96:97]
        else:
            state, mean = pltpu.roll(states, 96, 1), states[:, 32:33]
        mean = jnp.broadcast_to(mean, states.shape)
        state = jnp.where(lane >= 96, state, 0.0)
        maps[branch] = jnp.where(lane == 95, mean, state)
        parts = halves(tall(jnp.concatenate([state, mean], axis=1)))
        factor[branch] = jnp.concatenate(parts, axis=0)
    moves = [move(maps, maps_out, sems.at[0]), move(factor, factor_out, sems.at[1])]

    factors = (factor[0], factor[1])

    def step(i, carry):
        at = pl.multiple_of(i * 1024, 1024)
        found = []
        for branch, ref in enumerate((base, inner)):
            query, _, own = token_terms(ref[pl.ds(at, 1024), :], factors[branch])
            both_halves = jnp.concatenate(halves(own), axis=1)
            found.append(carry[branch] + mm(query, both_halves, (0, 0))[:HEAD])
        return tuple(found)

    zero = jnp.zeros((HEAD, 2 * LANES), F32)
    found = lax.fori_loop(0, base.shape[0] // 1024, step, (zero, zero))
    found = [pair[:, :LANES] + pair[:, LANES:] for pair in found]
    pack[...] = jnp.broadcast_to(pair_up(*found).astype(BF16)[None], pack.shape)
    moves.append(move(pack, pack_out, sems.at[2]))
    for copy in moves:
        copy.wait()


def query_kernel(
    base, inner, halo, both, maps_in, factor_in, q_out, att_out, halo_out, proj_out,
    maps, factor, q, att, halo_q, proj, sems,
):
    channels = both.shape[1] // 2
    first, second = move(maps_in, maps, sems.at[0]), move(factor_in, factor, sems.at[1])
    first.wait()
    second.wait()

    def query_grad(x, y, parts):
        high, low = halves(y)
        out = mm(jnp.concatenate([high, low], axis=1), parts[0], (1, 1)) + mm(high, parts[1], (1, 1))
        return jnp.where(x.astype(F32) > 0, out, 0.0).astype(BF16)

    parts, factors = [], []
    for branch in range(2):
        high, low = halves(tall(maps[branch]))
        parts.append((jnp.concatenate([high, high], axis=1), low))
        factors.append(factor[branch])

    def step(i, carry):
        at = pl.multiple_of(i * 1024, 1024)
        grads = both[pl.ds(at, 1024), channels:]
        found = []
        for branch, ref in enumerate((base, inner)):
            x = ref[pl.ds(at, 1024), :]
            _, out, y = token_terms(x, factors[branch])
            out = out.astype(BF16)
            att[branch, pl.ds(at, 1024), :] = out
            q[branch, pl.ds(at, 1024), :] = query_grad(x, y, parts[branch])
            found.append(carry[branch] + mm(out, grads, (0, 0))[96:])
        at = pl.multiple_of(i * 512, 512)
        x = halo[pl.ds(at, 512), :]
        halo_q[pl.ds(at, 512), :] = query_grad(x, token_terms(x, factors[1])[2], parts[1])
        return tuple(found)

    zero = jnp.zeros((HEAD, channels), F32)
    found = lax.fori_loop(0, base.shape[0] // 1024, step, (zero, zero))
    proj[0:HEAD] = found[0]
    proj[HEAD:] = found[1]
    moves = [
        move(q, q_out, sems.at[2]),
        move(att, att_out, sems.at[3]),
        move(halo_q, halo_out, sems.at[4]),
        move(proj, proj_out, sems.at[5]),
    ]
    for copy in moves:
        copy.wait()


def backward_kernel(
    total, gathered, base, inner, halo, kern, both, q_from, halo_from, att_from, strip_from, proj_from,
    weights_from, heads_from, own_from, slopes_from,
    tokens_out, att_out, parts, weights, proj_heads, own_tokens, own_grads, q_in, halo_q, att, strip, proj, field, straight, sums, sems,
):
    q_move = move(q_from, q_in, sems.at[0])
    halo_move = move(halo_from, halo_q, sems.at[1])
    att_move = move(att_from, att, sems.at[2])
    strip_move = move(strip_from, strip, sems.at[3])
    proj_move = move(proj_from, proj, sems.at[4])
    blank = jnp.zeros((weights.shape[0], HEAD, weights.shape[2]), BF16)
    weights[:, 3 * HEAD :] = blank
    proj_heads[:, :HEAD] = blank
    proj_heads[:, HEAD : 2 * HEAD] = blank
    later = [
        move(weights_from, weights.at[:, 0 : 3 * HEAD], sems.at[5]),
        move(heads_from, proj_heads.at[:, 2 * HEAD : LANES], sems.at[6]),
        move(own_from, own_tokens, sems.at[7]),
        move(slopes_from, own_grads, sems.at[8]),
    ]
    rows = strip.shape[0] - 2 * MARGIN
    cols = base.shape[0] // rows
    channels = both.shape[1] // 2
    grads = jnp.sum(gathered[...].astype(F32), axis=0) * (1.0 / total)
    lane = lane_of(grads.shape)

    def prepare(branch):
        if branch == 0:
            state, mean = pltpu.roll(grads, 96, 1), grads[:, 95:96]
        else:
            state, mean = pltpu.roll(grads, 32, 1), grads[:, 31:32]
        state = jnp.where((lane >= 64) & (lane < 96), state, 0.0)
        upper = jnp.where(lane == 96, jnp.broadcast_to(mean, state.shape), state)
        turned = pltpu.roll(jnp.transpose(tall(upper)), 32, 1)
        return jnp.concatenate(halves(turned + tall(state, HEAD)), axis=0)

    def masked(x, query_grad, factor):
        wide = x.astype(F32)
        spot = lane_of(wide.shape)
        left = jnp.where(spot < 64, relu(wide), jnp.where(spot < 96, wide, 1.0)).astype(BF16)
        out = mm(jnp.concatenate([left, left], axis=1), factor)
        keep = ((wide > 0) | (spot >= 64)) & (spot < 96)
        out = jnp.where(keep, out, 0.0).astype(BF16).astype(F32)
        return jnp.where(spot < HEAD, query_grad.astype(F32), out)

    base_factor, side_factor = prepare(0), prepare(1)
    edge = jnp.zeros((MARGIN,) + field.shape[1:], F32)
    field[0:MARGIN] = edge
    field[MARGIN + rows : rows + 2 * MARGIN] = edge
    wing = WING
    circle = lax.broadcasted_iota(jnp.int32, (wing, LANES), 0)
    shift = jnp.where(circle < 4, circle + cols, circle - wing)
    column = lax.axis_index("col") * cols + shift
    inside = (column >= 0) & (column < lax.axis_size("col") * cols)
    inside = inside & (shift >= -MARGIN) & (shift < cols + MARGIN)
    inside = inside[None]

    def make(i, carry):
        size = 64 * cols
        at = pl.multiple_of(i * size, size)
        out = masked(inner[pl.ds(at, size), :], q_in[1, pl.ds(at, size), :], side_factor)
        field[pl.ds(MARGIN + i * 64, 64), wing : wing + cols] = out.reshape(64, cols, LANES)
        out = masked(base[pl.ds(at, size), :], q_in[0, pl.ds(at, size), :], base_factor)
        straight[pl.ds(i * 64, 64)] = out.reshape(64, cols, LANES)
        size = 64 * wing
        at = pl.multiple_of(i * size, size)
        out = masked(halo[pl.ds(at, size), :], halo_q[pl.ds(at, size), :], side_factor)
        out = jnp.where(inside, out.reshape(64, wing, LANES), 0.0)
        field[pl.ds(MARGIN + i * 64, 64), 0:wing] = out
        field[pl.ds(MARGIN + i * 64, 64), wing + cols :] = out
        return carry

    q_move.wait()
    halo_move.wait()
    lax.fori_loop(0, rows // 64, make, 0)
    att_move.wait()
    strip_move.wait()
    proj_move.wait()
    step = 4

    def spread(i, carry):
        step = 8
        out = straight[pl.ds(i * step, step)]
        for b in range(TAPS):
            at = WING + MARGIN - b
            for a in range(TAPS):
                tap = kern[pl.ds(a * TAPS + b, 1), :].reshape(1, 1, LANES)
                window = field[pl.ds(i * step + 2 * MARGIN - a, step), at : at + cols]
                out = out + window * tap
        at = pl.multiple_of(i * step * cols, step * cols)
        size = step * cols
        out = out.reshape(size, LANES)
        out = jnp.where(lane_of(out.shape) < 96, out, att[0, pl.ds(at, size), :].astype(F32))
        tokens_out[pl.ds(at, size), :] = out.astype(BF16)
        return carry

    lax.fori_loop(0, rows // 8, spread, 0)

    def taps(i, carry):
        own = field[pl.ds(MARGIN + i * step, step), WING : WING + cols]
        found = list(carry)
        for b in range(TAPS):
            at = WING - MARGIN + b
            for a in range(TAPS):
                window = strip[pl.ds(i * step + a, step), at : at + cols]
                product = (window * own).reshape(step * cols // 8, 8, LANES)
                k = a * TAPS + b
                found[k] = found[k] + jnp.sum(product, axis=0)
        return tuple(found)

    zero = jnp.zeros((8, LANES), F32)
    found = lax.fori_loop(0, rows // step, taps, (zero,) * TAPS**2)
    sums[...] = jnp.zeros(sums.shape, F32)
    for k in range(TAPS**2):
        sums[k : k + 1, :] = jnp.sum(found[k], axis=0, keepdims=True)

    def outer(i, carry):
        at = pl.multiple_of(i * 1024, 1024)
        return carry + mm(tokens_out[pl.ds(at, 1024), :], both[pl.ds(at, 1024), :channels], (0, 0))

    weight = lax.fori_loop(0, rows * cols // 1024, outer, jnp.zeros((LANES, channels), F32))
    parts[0:96] = weight[:96, :LANES].astype(BF16)
    parts[96:192] = weight[:96, LANES:].astype(BF16)
    parts[192:256] = proj[:, :LANES].astype(BF16)
    parts[256:320] = proj[:, LANES:].astype(BF16)
    parts[320:352] = sums[...].astype(BF16)
    parts[352:384] = jnp.zeros((32, LANES), BF16)

    def pack(i, carry):
        at = pl.multiple_of(i * 128, 128)
        x = att[1, pl.ds(at, 128), :].astype(F32)
        out = jnp.zeros((32, LANES), F32)
        spot = lane_of(out.shape)
        for g in range(4):
            turned = pltpu.roll(x[32 * g : 32 * g + 32], (32 * g + 32) % LANES, 1)
            out = jnp.where((spot >= 32 * g) & (spot < 32 * g + 32), turned, out)
        att_out[i] = out.astype(BF16)
        return carry

    lax.fori_loop(0, rows // 8, pack, 0, unroll=True)
    for copy in later:
        copy.wait()


def finish_kernel(back, tokens, grads, weights, proj, block_out, input_out):
    heads = back.shape[0]
    mixed = []
    for h in range(heads):
        first = back[h, 0:128, :]
        packed = back[h, 128:160, :].astype(F32)
        side = jnp.concatenate([pltpu.roll(packed, 96 - 32 * g, 1) if g < 3 else packed for g in range(4)], axis=0)
        spot = lane_of(side.shape)
        both = jnp.where(spot >= 96, side, pltpu.roll(first.astype(F32), 96, 1))
        mixed.append(jnp.where(spot >= 64, both, 0.0).astype(BF16))
    attended = jnp.zeros(tokens.shape, F32)
    turned = jnp.zeros(tokens.shape, F32)
    for h in range(heads):
        turned = turned + mm(back[h, 0:128, :], weights[h])
        attended = attended + mm(mixed[h], proj[h])
    block_out[...] = (tokens[...].astype(F32) + attended).astype(BF16)
    input_out[...] = (grads[...].astype(F32) + turned).astype(BF16)


def assemble_kernel(sums, other, qkv_out, conv_out, proj_out, scratch, qkv_grad, conv_grad, proj_grad, sems):
    heads = sums.shape[1]
    core = lax.rem(lax.axis_index("col"), 2)
    for h in range(heads):
        for part in range(sums.shape[0]):
            at = pl.multiple_of(48 * part + 24 * core, 8)
            scratch[h, pl.ds(at, 24), :] = sums[part, h].astype(F32)
            at = pl.multiple_of(48 * part + 24 - 24 * core, 8)
            scratch[h, pl.ds(at, 24), :] = other[part, h].astype(F32)
    for h in range(heads):
        for branch in range(2):
            at = 256 * branch + 32 * h
            for half in range(2):
                row = 192 + 64 * half + 32 * branch
                proj_grad[at : at + 32, 128 * half : 128 * half + 128] = scratch[h, row : row + 32, :]
    moves = [move(proj_grad, proj_out, sems.at[0])]
    for half in range(2):
        for j in range(3):
            for quad in range(heads // 4):
                rows = [
                    scratch[4 * quad + h, 96 * half + 32 * j : 96 * half + 32 * j + 32, :]
                    for h in range(4)
                ]
                block = jnp.transpose(jnp.concatenate(rows, axis=0))
                at = 256 * j + 128 * quad
                qkv_grad[128 * half : 128 * half + 128, at : at + 128] = block
        at = 128 * half
        moves.append(move(qkv_grad.at[at : at + 128], qkv_out.at[at : at + 128], sems.at[1 + half]))
    for j in range(3):
        for quad in range(heads // 4):
            out = jnp.zeros((32, LANES), F32)
            spot = lane_of(out.shape)
            for h in range(4):
                turned = scratch[4 * quad + h, 320:352, :]
                if (h - j) % 4:
                    turned = pltpu.roll(turned, (32 * (h - j)) % LANES, 1)
                out = jnp.where((spot >= 32 * h) & (spot < 32 * h + 32), turned, out)
            at = 256 * j + 128 * quad
            conv_grad[:, at : at + 128] = out[: TAPS**2]
    moves.append(move(conv_grad, conv_out, sems.at[3]))
    for copy in moves:
        copy.wait()


def call(kernel, outs, near, far, scratch=(), sems=0, name=None, keep=True):
    vmem = pl.BlockSpec(memory_space=pltpu.VMEM)
    away = pl.BlockSpec(memory_space=pltpu.HBM)
    shapes, specs = [], []
    for shape, dtype, *flag in outs:
        if flag:
            shapes.append(pltpu.HBM(shape, dtype))
            specs.append(away)
        else:
            held = pltpu.VMEM(shape, dtype) if keep else jax.ShapeDtypeStruct(shape, dtype)
            shapes.append(held)
            specs.append(vmem)
    args = [pltpu.with_memory_space_constraint(arg, pltpu.VMEM) for arg in near]
    scratch = [pltpu.VMEM(shape, dtype) for shape, dtype, *_ in scratch]
    if sems:
        scratch.append(pltpu.SemaphoreType.DMA((sems,)))
    return pl.pallas_call(
        kernel,
        out_shape=shapes,
        in_specs=[vmem] * len(near) + [away] * len(far),
        out_specs=specs,
        scratch_shapes=scratch,
        compiler_params=pltpu.CompilerParams(vmem_limit_bytes=GRANT),
        name=name,
    )(*args, *[pltpu.with_memory_space_constraint(arg, pltpu.HBM) for arg in far])


def exchange(block, axis, groups=None):
    return lax.all_to_all(block, axis, 0, 0, tiled=True, axis_index_groups=groups)


def copies(block, count):
    return jnp.broadcast_to(block[None], (count,) + block.shape)


def local(tokens, qkv_weight, conv_weight, proj_weight, out_grad):
    height, cols, channels = tokens.shape
    heads = lax.axis_size("row")
    strips = lax.axis_size("col")
    head = lax.axis_index("row")
    place = lax.axis_index("col")
    rows = height * heads
    total = float(rows * cols * strips)
    count = rows * cols
    span = cols + 4 * MARGIN

    (spread,) = call(
        spread_kernel,
        [((heads, height, cols, 2 * channels), BF16, "away")],
        [],
        [tokens, out_grad],
        scratch=[((height, cols, 2 * channels), BF16)],
        sems=2 + heads,
        name="spread",
    )
    both = exchange(spread, "row")
    both = both.reshape(count, 2 * channels)

    qkv_heads = qkv_weight.reshape(channels, 3, heads, HEAD).transpose(2, 0, 1, 3)
    qkv_heads = qkv_heads.reshape(heads, channels, 3 * HEAD)
    own_qkv = lax.dynamic_index_in_dim(qkv_heads, head, 0, False)
    own_kernel = conv_weight.reshape(TAPS**2, 3, heads, HEAD)
    own_kernel = lax.dynamic_index_in_dim(own_kernel, head, 2, False).reshape(TAPS**2, 3 * HEAD)
    centre = (jnp.arange(TAPS**2) == TAPS**2 // 2).astype(F32)
    kern = jnp.concatenate(
        [own_kernel.astype(F32), jnp.broadcast_to(centre[:, None], (TAPS**2, HEAD))], axis=1
    )
    proj_heads = proj_weight.reshape(2, heads, HEAD, channels).transpose(1, 0, 2, 3)
    proj_heads = proj_heads.reshape(heads, 2 * HEAD, channels)
    own_proj = lax.dynamic_index_in_dim(proj_heads, head, 0, False)
    blank = jnp.zeros((channels, HEAD), BF16)
    blanks = jnp.zeros((channels, 3 * HEAD), BF16)
    upper = jnp.concatenate([own_qkv, blank], axis=1)
    side_map = jnp.concatenate([upper, jnp.concatenate([blanks, own_proj[HEAD:].T], axis=1)])
    base_map = jnp.concatenate([upper, jnp.concatenate([blanks, own_proj[:HEAD].T], axis=1)])
    sent = mm(both, side_map).astype(BF16).reshape(rows, cols, LANES)
    base = mm(both, base_map).astype(BF16)

    even = place % 2 == 0
    first, last = sent[:, :4], sent[:, cols - 4 :]
    apart = [(i, i + 1) for i in range(1, strips - 1, 2)]
    apart += [(j, i) for i, j in apart]
    beside = [(i, i ^ 1) for i in range(strips)]
    far = lax.ppermute(jnp.where(even, first, last), "col", apart)
    near = lax.ppermute(jnp.where(even, last, first), "col", beside)

    wings = rows * (span - cols)
    small = (strips, HEAD, LANES)
    tall_strip = ((rows + 2 * MARGIN, span + WING, LANES), F32, "away")
    inner, halo, strip, pack = call(
        aggregate_kernel,
        [((count, LANES), BF16), ((wings, LANES), BF16), tall_strip, (small, BF16)],
        [sent, near, far, base, kern],
        [],
        scratch=[((rows + 2 * MARGIN, span + 2 * WING, LANES), F32)],
        sems=1,
        name="aggregate",
    )
    gathered = exchange(pack, "col")
    terms = [((2, HEAD, LANES), F32, "away"), ((2, 2 * LANES, 2 * LANES), BF16, "away")]
    maps, factor, pack = call(
        lambda *refs: forward_kernel(total, *refs),
        terms + [(small, BF16, "away")],
        [gathered, base, inner],
        [],
        scratch=terms + [(small, BF16)],
        sems=3,
        name="forward",
    )
    gathered = exchange(pack, "col")
    tokens_shape = ((2, count, LANES), BF16, "away")
    parts = [
        tokens_shape,
        tokens_shape,
        ((wings, LANES), BF16, "away"),
        ((2 * HEAD, channels), F32, "away"),
    ]
    q, att, halo_q, proj = call(
        query_kernel,
        parts,
        [base, inner, halo, both],
        [maps, factor],
        scratch=terms + parts,
        sems=8,
        name="query",
    )
    tokens_out, att_out, parts, *held = call(
        lambda *refs: backward_kernel(total, *refs),
        [
            ((count, LANES), BF16),
            ((heads, 32, LANES), BF16),
            ((384, LANES), BF16),
            ((heads, LANES, channels), BF16),
            ((heads, LANES, channels), BF16),
            ((height * cols, channels), BF16),
            ((height * cols, channels), BF16),
        ],
        [gathered, base, inner, halo, kern, both],
        [
            q, halo_q, att, strip, proj, qkv_heads.transpose(0, 2, 1), proj_heads,
            tokens.reshape(-1, channels), out_grad.reshape(-1, channels),
        ],
        scratch=[
            tokens_shape,
            parts[2],
            tokens_shape,
            tall_strip,
            parts[3],
            tall_strip,
            ((rows, cols, LANES), F32),
            ((32, LANES), F32),
        ],
        sems=9,
        name="backward",
    )
    part = exchange(parts.reshape(strips, 24, LANES), "col")
    part = jnp.sum(part.astype(F32), axis=0).astype(BF16)
    sent_back = jnp.concatenate(
        [tokens_out.reshape(heads, -1, LANES), att_out, copies(part, heads)], axis=1
    )
    back = exchange(sent_back, "row")
    sums = back[:, 160:]
    groups = [[2 * i + c for i in range(strips // 2)] for c in range(2)]
    sums = exchange(copies(sums, strips // 2), "col", groups)
    weights, proj_rows, own_tokens, own_grads = held
    block_output, input_grad = call(
        finish_kernel,
        [((height * cols, channels), BF16)] * 2,
        [back, own_tokens, own_grads, weights, proj_rows],
        [],
        name="finish",
        keep=False,
    )
    other = lax.ppermute(sums, "col", beside)
    results = [
        ((channels, 3 * channels), F32, "away"),
        ((TAPS**2, 3 * channels), F32, "away"),
        ((2 * channels, channels), F32, "away"),
    ]
    qkv_grad, conv_grad, proj_grad = call(
        assemble_kernel,
        results,
        [sums, other],
        [],
        scratch=[((heads, 384, LANES), F32)] + results,
        sems=4,
        name="assemble",
    )
    return (
        block_output.reshape(tokens.shape),
        input_grad.reshape(tokens.shape),
        qkv_grad,
        conv_grad,
        proj_grad,
    )


def solution(mesh):
    placed = (P("row", "col", None), P(), P(), P(), P("row", "col", None))
    return jax.shard_map(
        local,
        mesh=mesh,
        in_specs=placed,
        out_specs=(P("row", "col", None), P("row", "col", None), P(), P(), P()),
        check_vma=False,
    )
```

```python
import jax
import jax.numpy as jnp
from jax import lax
from jax.experimental import pallas as pl
from jax.experimental.pallas import tpu as pltpu
from jax.sharding import PartitionSpec as P

HEAD = 32
TAPS = 5
MARGIN = TAPS // 2
LANES = 4 * HEAD
WING = 4 * MARGIN
GRANT = 16 * 2**20

F32 = jnp.float32
BF16 = jnp.bfloat16


def lane_of(shape):
    return lax.broadcasted_iota(jnp.int32, shape, len(shape) - 1)


def halves(x):
    high = x.astype(BF16)
    return high, (x - high.astype(F32)).astype(BF16)


def mm(left, right, contract=(1, 0)):
    dims = (((contract[0],), (contract[1],)), ((), ()))
    return lax.dot_general(left, right, dims, preferred_element_type=F32)


def relu(x):
    return jnp.maximum(x, jnp.zeros((), x.dtype))


def pair_up(base, side):
    lane = lane_of(base.shape)
    return jnp.where(lane < 64, pltpu.roll(side, 64, 1), base)


def tall(matrix, above=0):
    below = LANES - HEAD - above
    parts = [jnp.zeros((above, matrix.shape[1]), F32)] if above else []
    parts += [matrix, jnp.zeros((below, matrix.shape[1]), F32)]
    return jnp.concatenate(parts, axis=0)


def move(source, target, sem):
    copy = pltpu.make_async_copy(source, target, sem)
    copy.start()
    return copy


def spread_kernel(tokens, grads, out, buffer, sems):
    channels = tokens.shape[2]
    first = move(tokens, buffer.at[:, :, 0:channels], sems.at[0])
    second = move(grads, buffer.at[:, :, channels : 2 * channels], sems.at[1])
    first.wait()
    second.wait()
    moves = [move(buffer, out.at[i], sems.at[2 + i]) for i in range(out.shape[0])]
    for copy in moves:
        copy.wait()


def outer(x):
    ones = jnp.where(lane_of(x.shape) >= 96, jnp.ones((), BF16), x)
    return mm(relu(x), ones, (0, 0))[HEAD : 2 * HEAD]


def own_kernel_body(sent, base, kern, partial, base_sum, strip_out, strip, sems):
    rows, cols, _ = sent.shape
    span = cols + WING
    strip[...] = jnp.zeros(strip.shape, F32)
    strip[MARGIN : MARGIN + rows, WING : WING + cols] = sent[...].astype(F32)
    strip[MARGIN : MARGIN + rows, WING + span : 2 * WING + span] = sent[:, :WING].astype(F32)
    strip_move = move(strip.at[:, WING : WING + cols], strip_out, sems.at[0])
    step = 4

    def conv(i, carry):
        total = jnp.zeros((step, span, LANES), F32)
        for b in range(TAPS):
            at = WING - MARGIN + b
            for a in range(TAPS):
                tap = kern[pl.ds(a * TAPS + b, 1), :].reshape(1, 1, LANES)
                total = total + strip[pl.ds(i * step + a, step), at : at + span] * tap
        partial[pl.ds(i * step, step)] = total
        return carry

    lax.fori_loop(0, rows // step, conv, 0)
    base_sum[...] = outer(base[...])
    strip_move.wait()


def aggregate_kernel(partial, near, far, kern, base_sum, inner, halo, wings_out, pack, strip, sems):
    rows, span, _ = partial.shape
    cols = span - WING
    even = lax.rem(lax.axis_index("col"), 2) == 0
    low = jnp.where(even, far[...].astype(F32), near[...].astype(F32))
    high = jnp.where(even, near[...].astype(F32), far[...].astype(F32))
    strip[...] = jnp.zeros(strip.shape, F32)
    for at in (0, span):
        strip[MARGIN : MARGIN + rows, at : at + 4] = high
        strip[MARGIN : MARGIN + rows, at + 4 : at + 8] = low
    wings_move = move(strip.at[:, 0:WING], wings_out, sems.at[0])
    step = 4

    def conv(i, carry):
        pieces = []
        for start, taps in ((0, (0, 1)), (8, (3, 4)), (16, range(TAPS))):
            total = partial[pl.ds(i * step, step), start : start + 8]
            for b in taps:
                at = WING - MARGIN + b + start
                for a in range(TAPS):
                    tap = kern[pl.ds(a * TAPS + b, 1), :].reshape(1, 1, LANES)
                    total = total + strip[pl.ds(i * step + a, step), at : at + 8] * tap
            pieces.append(total)
        size = step * cols
        at = pl.multiple_of(i * size, size)
        whole = jnp.concatenate(pieces[:2], axis=1)
        inner[pl.ds(at, size), :] = whole.reshape(size, LANES).astype(BF16)
        size = step * WING
        at = pl.multiple_of(i * size, size)
        halo[pl.ds(at, size), :] = pieces[2].reshape(size, LANES).astype(BF16)
        return carry

    lax.fori_loop(0, rows // step, conv, 0)
    both_sums = pair_up(base_sum[...], outer(inner[...])).astype(BF16)
    pack[...] = jnp.broadcast_to(both_sums[None], pack.shape)
    wings_move.wait()


def token_terms(x, factor):
    query = relu(x)
    wide = x.astype(F32)
    spot = lane_of(wide.shape)
    products = mm(jnp.concatenate([query, query], axis=1), factor)
    numerator = products[:, :LANES]
    inverse = 1.0 / (products[:, LANES:] + 1.0)
    along = jnp.sum(jnp.where(spot >= 96, wide * numerator, 0.0), axis=1, keepdims=True)
    y = jnp.where(spot >= 96, wide * inverse, 0.0)
    y = jnp.where(spot == 95, -along * inverse * inverse, y)
    return query, numerator * inverse, y


def forward_kernel(total, gathered, base, inner, maps_out, factor_out, pack_out, maps, factor, pack, sems):
    states = jnp.sum(gathered[...].astype(F32), axis=0) * (1.0 / total)
    lane = lane_of(states.shape)
    for branch in range(2):
        if branch == 0:
            state, mean = pltpu.roll(states, 32, 1), states[:, 96:97]
        else:
            state, mean = pltpu.roll(states, 96, 1), states[:, 32:33]
        mean = jnp.broadcast_to(mean, states.shape)
        state = jnp.where(lane >= 96, state, 0.0)
        maps[branch] = jnp.where(lane == 95, mean, state)
        parts = halves(tall(jnp.concatenate([state, mean], axis=1)))
        factor[branch] = jnp.concatenate(parts, axis=0)
    moves = [move(maps, maps_out, sems.at[0]), move(factor, factor_out, sems.at[1])]

    factors = (factor[0], factor[1])

    def step(i, carry):
        at = pl.multiple_of(i * 1024, 1024)
        found = []
        for branch, ref in enumerate((base, inner)):
            query, _, own = token_terms(ref[pl.ds(at, 1024), :], factors[branch])
            both_halves = jnp.concatenate(halves(own), axis=1)
            found.append(carry[branch] + mm(query, both_halves, (0, 0))[:HEAD])
        return tuple(found)

    zero = jnp.zeros((HEAD, 2 * LANES), F32)
    found = lax.fori_loop(0, base.shape[0] // 1024, step, (zero, zero))
    found = [pair[:, :LANES] + pair[:, LANES:] for pair in found]
    pack[...] = jnp.broadcast_to(pair_up(*found).astype(BF16)[None], pack.shape)
    moves.append(move(pack, pack_out, sems.at[2]))
    for copy in moves:
        copy.wait()


def query_kernel(
    base, inner, halo, both, maps_in, factor_in, q_out, att_out, halo_out, proj_out,
    maps, factor, q, att, halo_q, proj, sems,
):
    channels = both.shape[1] // 2
    first, second = move(maps_in, maps, sems.at[0]), move(factor_in, factor, sems.at[1])
    first.wait()
    second.wait()

    def query_grad(x, y, parts):
        high, low = halves(y)
        out = mm(jnp.concatenate([high, low], axis=1), parts[0], (1, 1)) + mm(high, parts[1], (1, 1))
        return jnp.where(x.astype(F32) > 0, out, 0.0).astype(BF16)

    parts, factors = [], []
    for branch in range(2):
        high, low = halves(tall(maps[branch]))
        parts.append((jnp.concatenate([high, high], axis=1), low))
        factors.append(factor[branch])

    def step(i, carry):
        at = pl.multiple_of(i * 1024, 1024)
        grads = both[pl.ds(at, 1024), channels:]
        found = []
        for branch, ref in enumerate((base, inner)):
            x = ref[pl.ds(at, 1024), :]
            _, out, y = token_terms(x, factors[branch])
            out = out.astype(BF16)
            att[branch, pl.ds(at, 1024), :] = out
            q[branch, pl.ds(at, 1024), :] = query_grad(x, y, parts[branch])
            found.append(carry[branch] + mm(out, grads, (0, 0))[96:])
        at = pl.multiple_of(i * 512, 512)
        x = halo[pl.ds(at, 512), :]
        halo_q[pl.ds(at, 512), :] = query_grad(x, token_terms(x, factors[1])[2], parts[1])
        return tuple(found)

    zero = jnp.zeros((HEAD, channels), F32)
    found = lax.fori_loop(0, base.shape[0] // 1024, step, (zero, zero))
    proj[0:HEAD] = found[0]
    proj[HEAD:] = found[1]
    moves = [
        move(q, q_out, sems.at[2]),
        move(att, att_out, sems.at[3]),
        move(halo_q, halo_out, sems.at[4]),
        move(proj, proj_out, sems.at[5]),
    ]
    for copy in moves:
        copy.wait()


def backward_kernel(
    total, gathered, base, inner, halo, kern, both, q_from, halo_from, att_from, strip_from, proj_from, wings_from,
    weights_from, heads_from, own_from, slopes_from,
    tokens_out, att_out, parts, weights, proj_heads, own_tokens, own_grads, q_in, halo_q, att, strip, proj, field, straight, sums, sems,
):
    q_move = move(q_from, q_in, sems.at[0])
    halo_move = move(halo_from, halo_q, sems.at[1])
    att_move = move(att_from, att, sems.at[2])
    center = strip_from.shape[1]
    strip_moves = [
        move(strip_from, strip.at[:, WING : WING + center], sems.at[3]),
        move(wings_from, strip.at[:, 0:WING], sems.at[9]),
        move(wings_from, strip.at[:, WING + center : 2 * WING + center], sems.at[10]),
    ]
    proj_move = move(proj_from, proj, sems.at[4])
    blank = jnp.zeros((weights.shape[0], HEAD, weights.shape[2]), BF16)
    weights[:, 3 * HEAD :] = blank
    proj_heads[:, :HEAD] = blank
    proj_heads[:, HEAD : 2 * HEAD] = blank
    later = [
        move(weights_from, weights.at[:, 0 : 3 * HEAD], sems.at[5]),
        move(heads_from, proj_heads.at[:, 2 * HEAD : LANES], sems.at[6]),
        move(own_from, own_tokens, sems.at[7]),
        move(slopes_from, own_grads, sems.at[8]),
    ]
    rows = strip.shape[0] - 2 * MARGIN
    cols = base.shape[0] // rows
    channels = both.shape[1] // 2
    grads = jnp.sum(gathered[...].astype(F32), axis=0) * (1.0 / total)
    lane = lane_of(grads.shape)

    def prepare(branch):
        if branch == 0:
            state, mean = pltpu.roll(grads, 96, 1), grads[:, 95:96]
        else:
            state, mean = pltpu.roll(grads, 32, 1), grads[:, 31:32]
        state = jnp.where((lane >= 64) & (lane < 96), state, 0.0)
        upper = jnp.where(lane == 96, jnp.broadcast_to(mean, state.shape), state)
        turned = pltpu.roll(jnp.transpose(tall(upper)), 32, 1)
        return jnp.concatenate(halves(turned + tall(state, HEAD)), axis=0)

    def masked(x, query_grad, factor):
        wide = x.astype(F32)
        spot = lane_of(wide.shape)
        left = jnp.where(spot < 64, relu(wide), jnp.where(spot < 96, wide, 1.0)).astype(BF16)
        out = mm(jnp.concatenate([left, left], axis=1), factor)
        keep = ((wide > 0) | (spot >= 64)) & (spot < 96)
        out = jnp.where(keep, out, 0.0).astype(BF16).astype(F32)
        return jnp.where(spot < HEAD, query_grad.astype(F32), out)

    base_factor, side_factor = prepare(0), prepare(1)
    edge = jnp.zeros((MARGIN,) + field.shape[1:], F32)
    field[0:MARGIN] = edge
    field[MARGIN + rows : rows + 2 * MARGIN] = edge
    wing = WING
    circle = lax.broadcasted_iota(jnp.int32, (wing, LANES), 0)
    shift = jnp.where(circle < 4, circle + cols, circle - wing)
    column = lax.axis_index("col") * cols + shift
    inside = (column >= 0) & (column < lax.axis_size("col") * cols)
    inside = inside & (shift >= -MARGIN) & (shift < cols + MARGIN)
    inside = inside[None]

    def make(i, carry):
        size = 64 * cols
        at = pl.multiple_of(i * size, size)
        out = masked(inner[pl.ds(at, size), :], q_in[1, pl.ds(at, size), :], side_factor)
        field[pl.ds(MARGIN + i * 64, 64), wing : wing + cols] = out.reshape(64, cols, LANES)
        out = masked(base[pl.ds(at, size), :], q_in[0, pl.ds(at, size), :], base_factor)
        straight[pl.ds(i * 64, 64)] = out.reshape(64, cols, LANES)
        size = 64 * wing
        at = pl.multiple_of(i * size, size)
        out = masked(halo[pl.ds(at, size), :], halo_q[pl.ds(at, size), :], side_factor)
        out = jnp.where(inside, out.reshape(64, wing, LANES), 0.0)
        field[pl.ds(MARGIN + i * 64, 64), 0:wing] = out
        field[pl.ds(MARGIN + i * 64, 64), wing + cols :] = out
        return carry

    q_move.wait()
    halo_move.wait()
    lax.fori_loop(0, rows // 64, make, 0)
    att_move.wait()
    for copy in strip_moves:
        copy.wait()
    proj_move.wait()
    step = 4

    def spread(i, carry):
        step = 8
        out = straight[pl.ds(i * step, step)]
        for b in range(TAPS):
            at = WING + MARGIN - b
            for a in range(TAPS):
                tap = kern[pl.ds(a * TAPS + b, 1), :].reshape(1, 1, LANES)
                window = field[pl.ds(i * step + 2 * MARGIN - a, step), at : at + cols]
                out = out + window * tap
        at = pl.multiple_of(i * step * cols, step * cols)
        size = step * cols
        out = out.reshape(size, LANES)
        out = jnp.where(lane_of(out.shape) < 96, out, att[0, pl.ds(at, size), :].astype(F32))
        tokens_out[pl.ds(at, size), :] = out.astype(BF16)
        return carry

    lax.fori_loop(0, rows // 8, spread, 0)

    def taps(i, carry):
        own = field[pl.ds(MARGIN + i * step, step), WING : WING + cols]
        found = list(carry)
        for b in range(TAPS):
            at = WING - MARGIN + b
            for a in range(TAPS):
                window = strip[pl.ds(i * step + a, step), at : at + cols]
                product = (window * own).reshape(step * cols // 8, 8, LANES)
                k = a * TAPS + b
                found[k] = found[k] + jnp.sum(product, axis=0)
        return tuple(found)

    zero = jnp.zeros((8, LANES), F32)
    found = lax.fori_loop(0, rows // step, taps, (zero,) * TAPS**2)
    sums[...] = jnp.zeros(sums.shape, F32)
    for k in range(TAPS**2):
        sums[k : k + 1, :] = jnp.sum(found[k], axis=0, keepdims=True)

    def outer(i, carry):
        at = pl.multiple_of(i * 1024, 1024)
        return carry + mm(tokens_out[pl.ds(at, 1024), :], both[pl.ds(at, 1024), :channels], (0, 0))

    weight = lax.fori_loop(0, rows * cols // 1024, outer, jnp.zeros((LANES, channels), F32))
    parts[0:96] = weight[:96, :LANES].astype(BF16)
    parts[96:192] = weight[:96, LANES:].astype(BF16)
    parts[192:256] = proj[:, :LANES].astype(BF16)
    parts[256:320] = proj[:, LANES:].astype(BF16)
    parts[320:352] = sums[...].astype(BF16)
    parts[352:384] = jnp.zeros((32, LANES), BF16)

    def pack(i, carry):
        at = pl.multiple_of(i * 128, 128)
        x = att[1, pl.ds(at, 128), :].astype(F32)
        out = jnp.zeros((32, LANES), F32)
        spot = lane_of(out.shape)
        for g in range(4):
            turned = pltpu.roll(x[32 * g : 32 * g + 32], (32 * g + 32) % LANES, 1)
            out = jnp.where((spot >= 32 * g) & (spot < 32 * g + 32), turned, out)
        att_out[i] = out.astype(BF16)
        return carry

    lax.fori_loop(0, rows // 8, pack, 0, unroll=True)
    for copy in later:
        copy.wait()


def finish_kernel(back, tokens, grads, weights, proj, block_out, input_out):
    heads = back.shape[0]
    mixed = []
    for h in range(heads):
        first = back[h, 0:128, :]
        packed = back[h, 128:160, :].astype(F32)
        side = jnp.concatenate([pltpu.roll(packed, 96 - 32 * g, 1) if g < 3 else packed for g in range(4)], axis=0)
        spot = lane_of(side.shape)
        both = jnp.where(spot >= 96, side, pltpu.roll(first.astype(F32), 96, 1))
        mixed.append(jnp.where(spot >= 64, both, 0.0).astype(BF16))
    attended = jnp.zeros(tokens.shape, F32)
    turned = jnp.zeros(tokens.shape, F32)
    for h in range(heads):
        turned = turned + mm(back[h, 0:128, :], weights[h])
        attended = attended + mm(mixed[h], proj[h])
    block_out[...] = (tokens[...].astype(F32) + attended).astype(BF16)
    input_out[...] = (grads[...].astype(F32) + turned).astype(BF16)


def assemble_kernel(sums, other, qkv_out, conv_out, proj_out, scratch, qkv_grad, conv_grad, proj_grad, sems):
    heads = sums.shape[1]
    core = lax.rem(lax.axis_index("col"), 2)
    for h in range(heads):
        for part in range(sums.shape[0]):
            at = pl.multiple_of(48 * part + 24 * core, 8)
            scratch[h, pl.ds(at, 24), :] = sums[part, h].astype(F32)
            at = pl.multiple_of(48 * part + 24 - 24 * core, 8)
            scratch[h, pl.ds(at, 24), :] = other[part, h].astype(F32)
    for h in range(heads):
        for branch in range(2):
            at = 256 * branch + 32 * h
            for half in range(2):
                row = 192 + 64 * half + 32 * branch
                proj_grad[at : at + 32, 128 * half : 128 * half + 128] = scratch[h, row : row + 32, :]
    moves = [move(proj_grad, proj_out, sems.at[0])]
    for half in range(2):
        for j in range(3):
            for quad in range(heads // 4):
                rows = [
                    scratch[4 * quad + h, 96 * half + 32 * j : 96 * half + 32 * j + 32, :]
                    for h in range(4)
                ]
                block = jnp.transpose(jnp.concatenate(rows, axis=0))
                at = 256 * j + 128 * quad
                qkv_grad[128 * half : 128 * half + 128, at : at + 128] = block
        at = 128 * half
        moves.append(move(qkv_grad.at[at : at + 128], qkv_out.at[at : at + 128], sems.at[1 + half]))
    for j in range(3):
        for quad in range(heads // 4):
            out = jnp.zeros((32, LANES), F32)
            spot = lane_of(out.shape)
            for h in range(4):
                turned = scratch[4 * quad + h, 320:352, :]
                if (h - j) % 4:
                    turned = pltpu.roll(turned, (32 * (h - j)) % LANES, 1)
                out = jnp.where((spot >= 32 * h) & (spot < 32 * h + 32), turned, out)
            at = 256 * j + 128 * quad
            conv_grad[:, at : at + 128] = out[: TAPS**2]
    moves.append(move(conv_grad, conv_out, sems.at[3]))
    for copy in moves:
        copy.wait()


def call(kernel, outs, near, far, scratch=(), sems=0, name=None, keep=True):
    vmem = pl.BlockSpec(memory_space=pltpu.VMEM)
    away = pl.BlockSpec(memory_space=pltpu.HBM)
    shapes, specs = [], []
    for shape, dtype, *flag in outs:
        if flag:
            shapes.append(pltpu.HBM(shape, dtype))
            specs.append(away)
        else:
            held = pltpu.VMEM(shape, dtype) if keep else jax.ShapeDtypeStruct(shape, dtype)
            shapes.append(held)
            specs.append(vmem)
    args = [pltpu.with_memory_space_constraint(arg, pltpu.VMEM) for arg in near]
    scratch = [pltpu.VMEM(shape, dtype) for shape, dtype, *_ in scratch]
    if sems:
        scratch.append(pltpu.SemaphoreType.DMA((sems,)))
    return pl.pallas_call(
        kernel,
        out_shape=shapes,
        in_specs=[vmem] * len(near) + [away] * len(far),
        out_specs=specs,
        scratch_shapes=scratch,
        compiler_params=pltpu.CompilerParams(vmem_limit_bytes=GRANT),
        name=name,
    )(*args, *[pltpu.with_memory_space_constraint(arg, pltpu.HBM) for arg in far])


def exchange(block, axis, groups=None):
    return lax.all_to_all(block, axis, 0, 0, tiled=True, axis_index_groups=groups)


def copies(block, count):
    return jnp.broadcast_to(block[None], (count,) + block.shape)


def local(tokens, qkv_weight, conv_weight, proj_weight, out_grad):
    height, cols, channels = tokens.shape
    heads = lax.axis_size("row")
    strips = lax.axis_size("col")
    head = lax.axis_index("row")
    place = lax.axis_index("col")
    rows = height * heads
    total = float(rows * cols * strips)
    count = rows * cols
    span = cols + 4 * MARGIN

    (spread,) = call(
        spread_kernel,
        [((heads, height, cols, 2 * channels), BF16, "away")],
        [],
        [tokens, out_grad],
        scratch=[((height, cols, 2 * channels), BF16)],
        sems=2 + heads,
        name="spread",
    )
    both = exchange(spread, "row")
    both = both.reshape(count, 2 * channels)

    qkv_heads = qkv_weight.reshape(channels, 3, heads, HEAD).transpose(2, 0, 1, 3)
    qkv_heads = qkv_heads.reshape(heads, channels, 3 * HEAD)
    own_qkv = lax.dynamic_index_in_dim(qkv_heads, head, 0, False)
    own_kernel = conv_weight.reshape(TAPS**2, 3, heads, HEAD)
    own_kernel = lax.dynamic_index_in_dim(own_kernel, head, 2, False).reshape(TAPS**2, 3 * HEAD)
    centre = (jnp.arange(TAPS**2) == TAPS**2 // 2).astype(F32)
    kern = jnp.concatenate(
        [own_kernel.astype(F32), jnp.broadcast_to(centre[:, None], (TAPS**2, HEAD))], axis=1
    )
    proj_heads = proj_weight.reshape(2, heads, HEAD, channels).transpose(1, 0, 2, 3)
    proj_heads = proj_heads.reshape(heads, 2 * HEAD, channels)
    own_proj = lax.dynamic_index_in_dim(proj_heads, head, 0, False)
    blank = jnp.zeros((channels, HEAD), BF16)
    blanks = jnp.zeros((channels, 3 * HEAD), BF16)
    upper = jnp.concatenate([own_qkv, blank], axis=1)
    side_map = jnp.concatenate([upper, jnp.concatenate([blanks, own_proj[HEAD:].T], axis=1)])
    base_map = jnp.concatenate([upper, jnp.concatenate([blanks, own_proj[:HEAD].T], axis=1)])
    sent = mm(both, side_map).astype(BF16).reshape(rows, cols, LANES)
    base = mm(both, base_map).astype(BF16)

    even = place % 2 == 0
    first, last = sent[:, :4], sent[:, cols - 4 :]
    apart = [(i, i + 1) for i in range(1, strips - 1, 2)]
    apart += [(j, i) for i, j in apart]
    beside = [(i, i ^ 1) for i in range(strips)]
    far = lax.ppermute(jnp.where(even, first, last), "col", apart)
    near = lax.ppermute(jnp.where(even, last, first), "col", beside)

    wings = rows * (span - cols)
    small = (strips, HEAD, LANES)
    tall_strip = ((rows + 2 * MARGIN, span + WING, LANES), F32, "away")
    center_strip = ((rows + 2 * MARGIN, cols, LANES), F32, "away")
    wing_strip = ((rows + 2 * MARGIN, span - cols, LANES), F32, "away")
    full_strip = ((rows + 2 * MARGIN, span + 2 * WING, LANES), F32)
    partial, base_sum, strip = call(
        own_kernel_body,
        [((rows, span, LANES), F32), ((HEAD, LANES), F32), center_strip],
        [sent, base, kern],
        [],
        scratch=[full_strip],
        sems=1,
        name="own",
    )
    inner, halo, wings_strip, pack = call(
        aggregate_kernel,
        [((count, LANES), BF16), ((wings, LANES), BF16), wing_strip, (small, BF16)],
        [partial, near, far, kern, base_sum],
        [],
        scratch=[full_strip],
        sems=1,
        name="aggregate",
    )
    gathered = exchange(pack, "col")
    terms = [((2, HEAD, LANES), F32, "away"), ((2, 2 * LANES, 2 * LANES), BF16, "away")]
    maps, factor, pack = call(
        lambda *refs: forward_kernel(total, *refs),
        terms + [(small, BF16, "away")],
        [gathered, base, inner],
        [],
        scratch=terms + [(small, BF16)],
        sems=3,
        name="forward",
    )
    gathered = exchange(pack, "col")
    tokens_shape = ((2, count, LANES), BF16, "away")
    parts = [
        tokens_shape,
        tokens_shape,
        ((wings, LANES), BF16, "away"),
        ((2 * HEAD, channels), F32, "away"),
    ]
    q, att, halo_q, proj = call(
        query_kernel,
        parts,
        [base, inner, halo, both],
        [maps, factor],
        scratch=terms + parts,
        sems=8,
        name="query",
    )
    tokens_out, att_out, parts, *held = call(
        lambda *refs: backward_kernel(total, *refs),
        [
            ((count, LANES), BF16),
            ((heads, 32, LANES), BF16),
            ((384, LANES), BF16),
            ((heads, LANES, channels), BF16),
            ((heads, LANES, channels), BF16),
            ((height * cols, channels), BF16),
            ((height * cols, channels), BF16),
        ],
        [gathered, base, inner, halo, kern, both],
        [
            q, halo_q, att, strip, proj, wings_strip, qkv_heads.transpose(0, 2, 1), proj_heads,
            tokens.reshape(-1, channels), out_grad.reshape(-1, channels),
        ],
        scratch=[
            tokens_shape,
            parts[2],
            tokens_shape,
            tall_strip,
            parts[3],
            tall_strip,
            ((rows, cols, LANES), F32),
            ((32, LANES), F32),
        ],
        sems=11,
        name="backward",
    )
    part = exchange(parts.reshape(strips, 24, LANES), "col")
    part = jnp.sum(part.astype(F32), axis=0).astype(BF16)
    sent_back = jnp.concatenate(
        [tokens_out.reshape(heads, -1, LANES), att_out, copies(part, heads)], axis=1
    )
    back = exchange(sent_back, "row")
    sums = back[:, 160:]
    groups = [[2 * i + c for i in range(strips // 2)] for c in range(2)]
    sums = exchange(copies(sums, strips // 2), "col", groups)
    weights, proj_rows, own_tokens, own_grads = held
    block_output, input_grad = call(
        finish_kernel,
        [((height * cols, channels), BF16)] * 2,
        [back, own_tokens, own_grads, weights, proj_rows],
        [],
        name="finish",
        keep=False,
    )
    other = lax.ppermute(sums, "col", beside)
    results = [
        ((channels, 3 * channels), F32, "away"),
        ((TAPS**2, 3 * channels), F32, "away"),
        ((2 * channels, channels), F32, "away"),
    ]
    qkv_grad, conv_grad, proj_grad = call(
        assemble_kernel,
        results,
        [sums, other],
        [],
        scratch=[((heads, 384, LANES), F32)] + results,
        sems=4,
        name="assemble",
    )
    return (
        block_output.reshape(tokens.shape),
        input_grad.reshape(tokens.shape),
        qkv_grad,
        conv_grad,
        proj_grad,
    )


def solution(mesh):
    placed = (P("row", "col", None), P(), P(), P(), P("row", "col", None))
    return jax.shard_map(
        local,
        mesh=mesh,
        in_specs=placed,
        out_specs=(P("row", "col", None), P("row", "col", None), P(), P(), P()),
        check_vma=False,
    )
```

```python
import jax
import jax.numpy as jnp
from jax import lax
from jax.experimental import pallas as pl
from jax.experimental.pallas import tpu as pltpu
from jax.sharding import PartitionSpec as P

HEAD = 32
TAPS = 5
MARGIN = TAPS // 2
LANES = 4 * HEAD
LARGE = 3.0e38
WING = 4 * MARGIN
GRANT = 16 * 2**20

F32 = jnp.float32
BF16 = jnp.bfloat16


def lane_of(shape):
    return lax.broadcasted_iota(jnp.int32, shape, len(shape) - 1)


def halves(x):
    high = x.astype(BF16)
    return high, (x - high.astype(F32)).astype(BF16)


def mm(left, right, contract=(1, 0)):
    dims = (((contract[0],), (contract[1],)), ((), ()))
    return lax.dot_general(left, right, dims, preferred_element_type=F32)


def relu(x):
    return jnp.maximum(x, jnp.zeros((), x.dtype))


def pair_up(base, side):
    lane = lane_of(base.shape)
    return jnp.where(lane < 64, pltpu.roll(side, 64, 1), base)


def tall(matrix, above=0):
    below = LANES - HEAD - above
    parts = [jnp.zeros((above, matrix.shape[1]), F32)] if above else []
    parts += [matrix, jnp.zeros((below, matrix.shape[1]), F32)]
    return jnp.concatenate(parts, axis=0)


def move(source, target, sem):
    copy = pltpu.make_async_copy(source, target, sem)
    copy.start()
    return copy


def spread_kernel(tokens, grads, out, buffer, sems):
    channels = tokens.shape[2]
    first = move(tokens, buffer.at[:, :, 0:channels], sems.at[0])
    second = move(grads, buffer.at[:, :, channels : 2 * channels], sems.at[1])
    first.wait()
    second.wait()
    moves = [move(buffer, out.at[i], sems.at[2 + i]) for i in range(out.shape[0])]
    for copy in moves:
        copy.wait()


def outer(x):
    ones = jnp.where(lane_of(x.shape) >= 96, jnp.ones((), BF16), x)
    return mm(relu(x), ones, (0, 0))[HEAD : 2 * HEAD]


def own_kernel_body(sent, base, kern, partial, base_sum, strip_out, strip, sems):
    rows, cols, _ = sent.shape
    span = cols + WING
    strip[...] = jnp.zeros(strip.shape, F32)
    strip[MARGIN : MARGIN + rows, WING : WING + cols] = sent[...].astype(F32)
    strip[MARGIN : MARGIN + rows, WING + span : 2 * WING + span] = sent[:, :WING].astype(F32)
    strip_move = move(strip.at[:, WING : WING + cols], strip_out, sems.at[0])
    step = 4

    def conv(i, carry):
        total = jnp.zeros((step, span, LANES), F32)
        for b in range(TAPS):
            at = WING - MARGIN + b
            for a in range(TAPS):
                tap = kern[pl.ds(a * TAPS + b, 1), :].reshape(1, 1, LANES)
                total = total + strip[pl.ds(i * step + a, step), at : at + span] * tap
        partial[pl.ds(i * step, step)] = total
        return carry

    lax.fori_loop(0, rows // step, conv, 0)
    base_sum[...] = outer(base[...])
    strip_move.wait()


def aggregate_kernel(partial, near, far, kern, base_sum, inner, halo, wings_out, pack, strip, sems):
    rows, span, _ = partial.shape
    cols = span - WING
    even = lax.rem(lax.axis_index("col"), 2) == 0
    low = jnp.where(even, far[...].astype(F32), near[...].astype(F32))
    high = jnp.where(even, near[...].astype(F32), far[...].astype(F32))
    edge = jnp.zeros((MARGIN,) + strip.shape[1:], F32)
    strip[0:MARGIN] = edge
    strip[MARGIN + rows : rows + 2 * MARGIN] = edge
    strip[MARGIN : MARGIN + rows, WING:span] = jnp.zeros((rows, cols, LANES), F32)
    strip[MARGIN : MARGIN + rows, WING + span :] = jnp.zeros((rows, WING, LANES), F32)
    for at in (0, span):
        strip[MARGIN : MARGIN + rows, at : at + 4] = high
        strip[MARGIN : MARGIN + rows, at + 4 : at + 8] = low
    wings_move = move(strip.at[:, 0:WING], wings_out, sems.at[0])
    step = 4

    def conv(i, carry):
        pieces = []
        for start, taps in ((0, (0, 1)), (8, (3, 4)), (16, range(TAPS))):
            total = partial[pl.ds(i * step, step), start : start + 8]
            for b in taps:
                at = WING - MARGIN + b + start
                for a in range(TAPS):
                    tap = kern[pl.ds(a * TAPS + b, 1), :].reshape(1, 1, LANES)
                    total = total + strip[pl.ds(i * step + a, step), at : at + 8] * tap
            pieces.append(total)
        size = step * cols
        at = pl.multiple_of(i * size, size)
        whole = jnp.concatenate(pieces[:2], axis=1)
        inner[pl.ds(at, size), :] = whole.reshape(size, LANES).astype(BF16)
        size = step * WING
        at = pl.multiple_of(i * size, size)
        halo[pl.ds(at, size), :] = pieces[2].reshape(size, LANES).astype(BF16)
        return carry

    lax.fori_loop(0, rows // step, conv, 0)
    both_sums = pair_up(base_sum[...], outer(inner[...])).astype(BF16)
    pack[...] = jnp.broadcast_to(both_sums[None], pack.shape)
    wings_move.wait()


def token_terms(x, factor):
    query = relu(x)
    wide = x.astype(F32)
    spot = lane_of(wide.shape)
    products = mm(jnp.concatenate([query, query], axis=1), factor)
    numerator = products[:, :LANES]
    inverse = 1.0 / (products[:, LANES:] + 1.0)
    along = jnp.sum(wide * numerator, axis=1, keepdims=True)
    y = jnp.where(spot >= 96, wide * inverse, 0.0)
    y = jnp.where(spot == 95, -along * inverse * inverse, y)
    return query, numerator * inverse, y


def forward_kernel(total, gathered, base, inner, maps_out, factor_out, pack_out, maps, factor, pack, sems):
    states = jnp.sum(gathered[...].astype(F32), axis=0) * (1.0 / total)
    lane = lane_of(states.shape)
    for branch in range(2):
        if branch == 0:
            state, mean = pltpu.roll(states, 32, 1), states[:, 96:97]
        else:
            state, mean = pltpu.roll(states, 96, 1), states[:, 32:33]
        mean = jnp.broadcast_to(mean, states.shape)
        state = jnp.where(lane >= 96, state, 0.0)
        maps[branch] = jnp.where(lane == 95, mean, state)
        parts = halves(tall(jnp.concatenate([state, mean], axis=1)))
        factor[branch] = jnp.concatenate(parts, axis=0)
    moves = [move(maps, maps_out, sems.at[0]), move(factor, factor_out, sems.at[1])]

    factors = (factor[0], factor[1])

    def step(i, carry):
        at = pl.multiple_of(i * 1024, 1024)
        found = []
        for branch, ref in enumerate((base, inner)):
            query, _, own = token_terms(ref[pl.ds(at, 1024), :], factors[branch])
            both_halves = jnp.concatenate(halves(own), axis=1)
            found.append(carry[branch] + mm(query, both_halves, (0, 0))[:HEAD])
        return tuple(found)

    zero = jnp.zeros((HEAD, 2 * LANES), F32)
    found = lax.fori_loop(0, base.shape[0] // 1024, step, (zero, zero))
    found = [pair[:, :LANES] + pair[:, LANES:] for pair in found]
    pack[...] = jnp.broadcast_to(pair_up(*found).astype(BF16)[None], pack.shape)
    moves.append(move(pack, pack_out, sems.at[2]))
    for copy in moves:
        copy.wait()


def query_kernel(
    base, inner, halo, both, maps_in, factor_in, q_out, att_out, halo_out, proj_out,
    maps, factor, q, att, halo_q, proj, sems,
):
    channels = both.shape[1] // 2
    first, second = move(maps_in, maps, sems.at[0]), move(factor_in, factor, sems.at[1])
    first.wait()
    second.wait()

    def query_grad(x, y, parts):
        high, low = halves(y)
        out = mm(jnp.concatenate([high, low], axis=1), parts[0], (1, 1)) + mm(high, parts[1], (1, 1))
        return jnp.where(x.astype(F32) > 0, out, 0.0).astype(BF16)

    parts, factors = [], []
    for branch in range(2):
        high, low = halves(tall(maps[branch]))
        parts.append((jnp.concatenate([high, high], axis=1), low))
        factors.append(factor[branch])

    def step(i, carry):
        at = pl.multiple_of(i * 1024, 1024)
        grads = both[pl.ds(at, 1024), channels:]
        found = []
        for branch, ref in enumerate((base, inner)):
            x = ref[pl.ds(at, 1024), :]
            _, out, y = token_terms(x, factors[branch])
            out = out.astype(BF16)
            att[branch, pl.ds(at, 1024), :] = out
            q[branch, pl.ds(at, 1024), :] = query_grad(x, y, parts[branch])
            found.append(carry[branch] + mm(out, grads, (0, 0))[96:])
        at = pl.multiple_of(i * 512, 512)
        x = halo[pl.ds(at, 512), :]
        halo_q[pl.ds(at, 512), :] = query_grad(x, token_terms(x, factors[1])[2], parts[1])
        return tuple(found)

    zero = jnp.zeros((HEAD, channels), F32)
    found = lax.fori_loop(0, base.shape[0] // 1024, step, (zero, zero))
    proj[0:HEAD] = found[0]
    proj[HEAD:] = found[1]
    moves = [
        move(q, q_out, sems.at[2]),
        move(att, att_out, sems.at[3]),
        move(halo_q, halo_out, sems.at[4]),
        move(proj, proj_out, sems.at[5]),
    ]
    for copy in moves:
        copy.wait()


def backward_kernel(
    total, gathered, base, inner, halo, kern, both, q_from, halo_from, att_from, strip_from, proj_from, wings_from,
    weights_from, heads_from, own_from, slopes_from,
    tokens_out, att_out, parts, weights, proj_heads, own_tokens, own_grads, q_in, halo_q, att, strip, proj, field, straight, sums, sems,
):
    q_move = move(q_from, q_in, sems.at[0])
    halo_move = move(halo_from, halo_q, sems.at[1])
    att_move = move(att_from, att, sems.at[2])
    center = strip_from.shape[1]
    strip_moves = [
        move(strip_from, strip.at[:, WING : WING + center], sems.at[3]),
        move(wings_from, strip.at[:, 0:WING], sems.at[9]),
        move(wings_from, strip.at[:, WING + center : 2 * WING + center], sems.at[10]),
    ]
    proj_move = move(proj_from, proj, sems.at[4])
    blank = jnp.zeros((weights.shape[0], HEAD, weights.shape[2]), BF16)
    weights[:, 3 * HEAD :] = blank
    proj_heads[:, :HEAD] = blank
    proj_heads[:, HEAD : 2 * HEAD] = blank
    later = [
        move(weights_from, weights.at[:, 0 : 3 * HEAD], sems.at[5]),
        move(heads_from, proj_heads.at[:, 2 * HEAD : LANES], sems.at[6]),
        move(own_from, own_tokens, sems.at[7]),
        move(slopes_from, own_grads, sems.at[8]),
    ]
    rows = strip.shape[0] - 2 * MARGIN
    cols = base.shape[0] // rows
    channels = both.shape[1] // 2
    grads = jnp.sum(gathered[...].astype(F32), axis=0) * (1.0 / total)
    lane = lane_of(grads.shape)

    def prepare(branch):
        if branch == 0:
            state, mean = pltpu.roll(grads, 96, 1), grads[:, 95:96]
        else:
            state, mean = pltpu.roll(grads, 32, 1), grads[:, 31:32]
        state = jnp.where((lane >= 64) & (lane < 96), state, 0.0)
        upper = jnp.where(lane == 96, jnp.broadcast_to(mean, state.shape), state)
        turned = pltpu.roll(jnp.transpose(tall(upper)), 32, 1)
        return jnp.concatenate(halves(turned + tall(state, HEAD)), axis=0)

    spot = lane_of((1, LANES))
    least = jnp.where(spot < 64, 0.0, jnp.where(spot < 96, -LARGE, 1.0)).astype(BF16)
    most = jnp.where(spot < 96, LARGE, 1.0).astype(BF16)
    bar = jnp.where(spot < 64, 0.0, -LARGE)

    def masked(x, query_grad, factor):
        left = jnp.minimum(jnp.maximum(x, least), most)
        out = mm(jnp.concatenate([left, left], axis=1), factor)
        out = jnp.where(x.astype(F32) > bar, out, 0.0).astype(BF16).astype(F32)
        return out + query_grad.astype(F32)

    base_factor, side_factor = prepare(0), prepare(1)
    edge = jnp.zeros((MARGIN,) + field.shape[1:], F32)
    field[0:MARGIN] = edge
    field[MARGIN + rows : rows + 2 * MARGIN] = edge
    wing = WING
    circle = lax.broadcasted_iota(jnp.int32, (wing, LANES), 0)
    shift = jnp.where(circle < 4, circle + cols, circle - wing)
    column = lax.axis_index("col") * cols + shift
    inside = (column >= 0) & (column < lax.axis_size("col") * cols)
    inside = inside & (shift >= -MARGIN) & (shift < cols + MARGIN)
    inside = inside[None]

    def make(i, carry):
        size = 64 * cols
        at = pl.multiple_of(i * size, size)
        out = masked(inner[pl.ds(at, size), :], q_in[1, pl.ds(at, size), :], side_factor)
        field[pl.ds(MARGIN + i * 64, 64), wing : wing + cols] = out.reshape(64, cols, LANES)
        out = masked(base[pl.ds(at, size), :], q_in[0, pl.ds(at, size), :], base_factor)
        straight[pl.ds(i * 64, 64)] = out.reshape(64, cols, LANES)
        size = 64 * wing
        at = pl.multiple_of(i * size, size)
        out = masked(halo[pl.ds(at, size), :], halo_q[pl.ds(at, size), :], side_factor)
        out = jnp.where(inside, out.reshape(64, wing, LANES), 0.0)
        field[pl.ds(MARGIN + i * 64, 64), 0:wing] = out
        field[pl.ds(MARGIN + i * 64, 64), wing + cols :] = out
        return carry

    q_move.wait()
    halo_move.wait()
    lax.fori_loop(0, rows // 64, make, 0)
    att_move.wait()
    for copy in strip_moves:
        copy.wait()
    proj_move.wait()
    step = 4

    def spread(i, carry):
        out = straight[pl.ds(i * step, step)]
        for b in range(TAPS):
            at = WING + MARGIN - b
            for a in range(TAPS):
                tap = kern[pl.ds(a * TAPS + b, 1), :].reshape(1, 1, LANES)
                window = field[pl.ds(i * step + 2 * MARGIN - a, step), at : at + cols]
                out = out + window * tap
        at = pl.multiple_of(i * step * cols, step * cols)
        size = step * cols
        out = out.reshape(size, LANES)
        out = jnp.where(lane_of(out.shape) < 96, out, att[0, pl.ds(at, size), :].astype(F32))
        tokens_out[pl.ds(at, size), :] = out.astype(BF16)
        return carry

    lax.fori_loop(0, rows // step, spread, 0)

    def taps(i, carry):
        own = field[pl.ds(MARGIN + i * step, step), WING : WING + cols]
        found = list(carry)
        for b in range(TAPS):
            at = WING - MARGIN + b
            for a in range(TAPS):
                window = strip[pl.ds(i * step + a, step), at : at + cols]
                product = (window * own).reshape(step * cols // 8, 8, LANES)
                k = a * TAPS + b
                found[k] = found[k] + jnp.sum(product, axis=0)
        return tuple(found)

    zero = jnp.zeros((8, LANES), F32)
    found = lax.fori_loop(0, rows // step, taps, (zero,) * TAPS**2)
    sums[...] = jnp.zeros(sums.shape, F32)
    for k in range(TAPS**2):
        sums[k : k + 1, :] = jnp.sum(found[k], axis=0, keepdims=True)

    def outer(i, carry):
        at = pl.multiple_of(i * 1024, 1024)
        return carry + mm(tokens_out[pl.ds(at, 1024), :], both[pl.ds(at, 1024), :channels], (0, 0))

    weight = lax.fori_loop(0, rows * cols // 1024, outer, jnp.zeros((LANES, channels), F32))
    parts[0:96] = weight[:96, :LANES].astype(BF16)
    parts[96:192] = weight[:96, LANES:].astype(BF16)
    parts[192:256] = proj[:, :LANES].astype(BF16)
    parts[256:320] = proj[:, LANES:].astype(BF16)
    parts[320:352] = sums[...].astype(BF16)
    parts[352:384] = jnp.zeros((32, LANES), BF16)

    def pack(i, carry):
        at = pl.multiple_of(i * 128, 128)
        x = att[1, pl.ds(at, 128), :].astype(F32)
        out = jnp.zeros((32, LANES), F32)
        spot = lane_of(out.shape)
        for g in range(4):
            turned = pltpu.roll(x[32 * g : 32 * g + 32], (32 * g + 32) % LANES, 1)
            out = jnp.where((spot >= 32 * g) & (spot < 32 * g + 32), turned, out)
        att_out[i] = out.astype(BF16)
        return carry

    lax.fori_loop(0, rows // 8, pack, 0, unroll=True)
    for copy in later:
        copy.wait()


def finish_kernel(back, tokens, grads, weights, proj, block_out, input_out):
    heads = back.shape[0]
    mixed = []
    for h in range(heads):
        first = back[h, 0:128, :]
        packed = back[h, 128:160, :].astype(F32)
        side = jnp.concatenate([pltpu.roll(packed, 96 - 32 * g, 1) if g < 3 else packed for g in range(4)], axis=0)
        spot = lane_of(side.shape)
        both = jnp.where(spot >= 96, side, pltpu.roll(first.astype(F32), 96, 1))
        mixed.append(jnp.where(spot >= 64, both, 0.0).astype(BF16))
    attended = jnp.zeros(tokens.shape, F32)
    turned = jnp.zeros(tokens.shape, F32)
    for h in range(heads):
        turned = turned + mm(back[h, 0:128, :], weights[h])
        attended = attended + mm(mixed[h], proj[h])
    block_out[...] = (tokens[...].astype(F32) + attended).astype(BF16)
    input_out[...] = (grads[...].astype(F32) + turned).astype(BF16)


def assemble_kernel(sums, other, qkv_out, conv_out, proj_out, scratch, qkv_grad, conv_grad, proj_grad, sems):
    heads = sums.shape[1]
    core = lax.rem(lax.axis_index("col"), 2)
    for h in range(heads):
        for part in range(sums.shape[0]):
            at = pl.multiple_of(48 * part + 24 * core, 8)
            scratch[h, pl.ds(at, 24), :] = sums[part, h].astype(F32)
            at = pl.multiple_of(48 * part + 24 - 24 * core, 8)
            scratch[h, pl.ds(at, 24), :] = other[part, h].astype(F32)
    for h in range(heads):
        for branch in range(2):
            at = 256 * branch + 32 * h
            for half in range(2):
                row = 192 + 64 * half + 32 * branch
                proj_grad[at : at + 32, 128 * half : 128 * half + 128] = scratch[h, row : row + 32, :]
    moves = [move(proj_grad, proj_out, sems.at[0])]
    for half in range(2):
        for j in range(3):
            for quad in range(heads // 4):
                rows = [
                    scratch[4 * quad + h, 96 * half + 32 * j : 96 * half + 32 * j + 32, :]
                    for h in range(4)
                ]
                block = jnp.transpose(jnp.concatenate(rows, axis=0))
                at = 256 * j + 128 * quad
                qkv_grad[128 * half : 128 * half + 128, at : at + 128] = block
        at = 128 * half
        moves.append(move(qkv_grad.at[at : at + 128], qkv_out.at[at : at + 128], sems.at[1 + half]))
    for j in range(3):
        for quad in range(heads // 4):
            out = jnp.zeros((32, LANES), F32)
            spot = lane_of(out.shape)
            for h in range(4):
                turned = scratch[4 * quad + h, 320:352, :]
                if (h - j) % 4:
                    turned = pltpu.roll(turned, (32 * (h - j)) % LANES, 1)
                out = jnp.where((spot >= 32 * h) & (spot < 32 * h + 32), turned, out)
            at = 256 * j + 128 * quad
            conv_grad[:, at : at + 128] = out[: TAPS**2]
    moves.append(move(conv_grad, conv_out, sems.at[3]))
    for copy in moves:
        copy.wait()


def call(kernel, outs, near, far, scratch=(), sems=0, name=None, keep=True):
    vmem = pl.BlockSpec(memory_space=pltpu.VMEM)
    away = pl.BlockSpec(memory_space=pltpu.HBM)
    shapes, specs = [], []
    for shape, dtype, *flag in outs:
        if flag:
            shapes.append(pltpu.HBM(shape, dtype))
            specs.append(away)
        else:
            held = pltpu.VMEM(shape, dtype) if keep else jax.ShapeDtypeStruct(shape, dtype)
            shapes.append(held)
            specs.append(vmem)
    args = [pltpu.with_memory_space_constraint(arg, pltpu.VMEM) for arg in near]
    scratch = [pltpu.VMEM(shape, dtype) for shape, dtype, *_ in scratch]
    if sems:
        scratch.append(pltpu.SemaphoreType.DMA((sems,)))
    return pl.pallas_call(
        kernel,
        out_shape=shapes,
        in_specs=[vmem] * len(near) + [away] * len(far),
        out_specs=specs,
        scratch_shapes=scratch,
        compiler_params=pltpu.CompilerParams(vmem_limit_bytes=GRANT),
        name=name,
    )(*args, *[pltpu.with_memory_space_constraint(arg, pltpu.HBM) for arg in far])


def exchange(block, axis, groups=None):
    return lax.all_to_all(block, axis, 0, 0, tiled=True, axis_index_groups=groups)


def copies(block, count):
    return jnp.broadcast_to(block[None], (count,) + block.shape)


def local(tokens, qkv_weight, conv_weight, proj_weight, out_grad):
    height, cols, channels = tokens.shape
    heads = lax.axis_size("row")
    strips = lax.axis_size("col")
    head = lax.axis_index("row")
    place = lax.axis_index("col")
    rows = height * heads
    total = float(rows * cols * strips)
    count = rows * cols
    span = cols + 4 * MARGIN

    (spread,) = call(
        spread_kernel,
        [((heads, height, cols, 2 * channels), BF16, "away")],
        [],
        [tokens, out_grad],
        scratch=[((height, cols, 2 * channels), BF16)],
        sems=2 + heads,
        name="spread",
    )
    both = exchange(spread, "row")
    both = both.reshape(count, 2 * channels)

    qkv_heads = qkv_weight.reshape(channels, 3, heads, HEAD).transpose(2, 0, 1, 3)
    qkv_heads = qkv_heads.reshape(heads, channels, 3 * HEAD)
    own_qkv = lax.dynamic_index_in_dim(qkv_heads, head, 0, False)
    own_kernel = conv_weight.reshape(TAPS**2, 3, heads, HEAD)
    own_kernel = lax.dynamic_index_in_dim(own_kernel, head, 2, False).reshape(TAPS**2, 3 * HEAD)
    centre = (jnp.arange(TAPS**2) == TAPS**2 // 2).astype(F32)
    kern = jnp.concatenate(
        [own_kernel.astype(F32), jnp.broadcast_to(centre[:, None], (TAPS**2, HEAD))], axis=1
    )
    proj_heads = proj_weight.reshape(2, heads, HEAD, channels).transpose(1, 0, 2, 3)
    proj_heads = proj_heads.reshape(heads, 2 * HEAD, channels)
    own_proj = lax.dynamic_index_in_dim(proj_heads, head, 0, False)
    blank = jnp.zeros((channels, HEAD), BF16)
    blanks = jnp.zeros((channels, 3 * HEAD), BF16)
    upper = jnp.concatenate([own_qkv, blank], axis=1)
    side_map = jnp.concatenate([upper, jnp.concatenate([blanks, own_proj[HEAD:].T], axis=1)])
    base_map = jnp.concatenate([upper, jnp.concatenate([blanks, own_proj[:HEAD].T], axis=1)])
    sent = mm(both, side_map).astype(BF16).reshape(rows, cols, LANES)
    base = mm(both, base_map).astype(BF16)

    even = place % 2 == 0
    first, last = sent[:, :4], sent[:, cols - 4 :]
    apart = [(i, i + 1) for i in range(1, strips - 1, 2)]
    apart += [(j, i) for i, j in apart]
    beside = [(i, i ^ 1) for i in range(strips)]
    far = lax.ppermute(jnp.where(even, first, last), "col", apart)
    near = lax.ppermute(jnp.where(even, last, first), "col", beside)

    wings = rows * (span - cols)
    small = (strips, HEAD, LANES)
    tall_strip = ((rows + 2 * MARGIN, span + WING, LANES), F32, "away")
    center_strip = ((rows + 2 * MARGIN, cols, LANES), F32, "away")
    wing_strip = ((rows + 2 * MARGIN, span - cols, LANES), F32, "away")
    full_strip = ((rows + 2 * MARGIN, span + 2 * WING, LANES), F32)
    partial, base_sum, strip = call(
        own_kernel_body,
        [((rows, span, LANES), F32), ((HEAD, LANES), F32), center_strip],
        [sent, base, kern],
        [],
        scratch=[full_strip],
        sems=1,
        name="own",
    )
    inner, halo, wings_strip, pack = call(
        aggregate_kernel,
        [((count, LANES), BF16), ((wings, LANES), BF16), wing_strip, (small, BF16)],
        [partial, near, far, kern, base_sum],
        [],
        scratch=[full_strip],
        sems=1,
        name="aggregate",
    )
    gathered = exchange(pack, "col")
    terms = [((2, HEAD, LANES), F32, "away"), ((2, 2 * LANES, 2 * LANES), BF16, "away")]
    maps, factor, pack = call(
        lambda *refs: forward_kernel(total, *refs),
        terms + [(small, BF16, "away")],
        [gathered, base, inner],
        [],
        scratch=terms + [(small, BF16)],
        sems=3,
        name="forward",
    )
    gathered = exchange(pack, "col")
    tokens_shape = ((2, count, LANES), BF16, "away")
    parts = [
        tokens_shape,
        tokens_shape,
        ((wings, LANES), BF16, "away"),
        ((2 * HEAD, channels), F32, "away"),
    ]
    q, att, halo_q, proj = call(
        query_kernel,
        parts,
        [base, inner, halo, both],
        [maps, factor],
        scratch=terms + parts,
        sems=8,
        name="query",
    )
    tokens_out, att_out, parts, *held = call(
        lambda *refs: backward_kernel(total, *refs),
        [
            ((count, LANES), BF16),
            ((heads, 32, LANES), BF16),
            ((384, LANES), BF16),
            ((heads, LANES, channels), BF16),
            ((heads, LANES, channels), BF16),
            ((height * cols, channels), BF16),
            ((height * cols, channels), BF16),
        ],
        [gathered, base, inner, halo, kern, both],
        [
            q, halo_q, att, strip, proj, wings_strip, qkv_heads.transpose(0, 2, 1), proj_heads,
            tokens.reshape(-1, channels), out_grad.reshape(-1, channels),
        ],
        scratch=[
            tokens_shape,
            parts[2],
            tokens_shape,
            tall_strip,
            parts[3],
            tall_strip,
            ((rows, cols, LANES), F32),
            ((32, LANES), F32),
        ],
        sems=11,
        name="backward",
    )
    part = exchange(parts.reshape(strips, 24, LANES), "col")
    part = jnp.sum(part.astype(F32), axis=0).astype(BF16)
    sent_back = jnp.concatenate(
        [tokens_out.reshape(heads, -1, LANES), att_out, copies(part, heads)], axis=1
    )
    back = exchange(sent_back, "row")
    sums = back[:, 160:]
    groups = [[2 * i + c for i in range(strips // 2)] for c in range(2)]
    sums = exchange(copies(sums, strips // 2), "col", groups)
    weights, proj_rows, own_tokens, own_grads = held
    block_output, input_grad = call(
        finish_kernel,
        [((height * cols, channels), BF16)] * 2,
        [back, own_tokens, own_grads, weights, proj_rows],
        [],
        name="finish",
        keep=False,
    )
    other = lax.ppermute(sums, "col", beside)
    results = [
        ((channels, 3 * channels), F32, "away"),
        ((TAPS**2, 3 * channels), F32, "away"),
        ((2 * channels, channels), F32, "away"),
    ]
    qkv_grad, conv_grad, proj_grad = call(
        assemble_kernel,
        results,
        [sums, other],
        [],
        scratch=[((heads, 384, LANES), F32)] + results,
        sems=4,
        name="assemble",
    )
    return (
        block_output.reshape(tokens.shape),
        input_grad.reshape(tokens.shape),
        qkv_grad,
        conv_grad,
        proj_grad,
    )


def solution(mesh):
    placed = (P("row", "col", None), P(), P(), P(), P("row", "col", None))
    return jax.shard_map(
        local,
        mesh=mesh,
        in_specs=placed,
        out_specs=(P("row", "col", None), P("row", "col", None), P(), P(), P()),
        check_vma=False,
    )
```
